256 devices in a mesh: branch: 2 (over x_hi), row: 16 (over z, core), chan: 8 (over x_lo, y).
Axes of the slice: x: 4 (x_hi: 2, x_lo: 2; x = x_hi * 2 + x_lo), y: 4, z: 8, core: 2. Of those that a mesh axis runs over, the one named last changes fastest.
Arguments:
- homolog_stack: bfloat16 [256, 1024, 256], P(('branch', 'row'), 'chan'), may hold values from -6 to 6
- couple_tensor: bfloat16 [1024, 1024, 128], P(('branch', 'row'), 'chan'), may hold values from -6 to 6
- amino_occupancy: int32 [1024], replicated, may hold values 0 or 1
- homolog_occupancy: int32 [256, 1024], P(('branch', 'row'), 'chan'), may hold values 0 or 1
- focus_entry_coefficients: bfloat16 [256, 1024], replicated, may hold values from -0.375 to 0.375
- couple_offset_coefficients: bfloat16 [128, 8], replicated, may hold values from -0.5 to 0.5
- focus_exit_coefficients: bfloat16 [256, 256], replicated, may hold values from -0.375 to 0.375
- tensor_entry_coefficients: bfloat16 [256, 64], replicated, may hold values from -0.375 to 0.375
- tensor_exit_coefficients: bfloat16 [1024, 128], replicated, may hold values from -1 to 1
- trio_entry_coefficients: bfloat16 [128, 512], replicated, may hold values from -0.5 to 0.5
- trio_exit_switch: bfloat16 [128, 128], replicated, may hold values from -0.5 to 0.5
- trio_exit_coefficients: bfloat16 [128, 128], replicated, may hold values from -0.5 to 0.5
Outputs:
- homolog_after_update: bfloat16 [256, 1024, 256], P(('branch', 'row'), 'chan')
- pair_result: bfloat16 [1024, 1024, 128], P(('branch', 'row'), 'chan')
The draws below stay inside these ranges and needn't reach their ends.
All inputs are finite; a program needn't handle non-finite values. No bound on the sum of `homolog_occupancy` on one device may be relied on, other than what follows from the above.
Results may differ from the reference program's by a relative error of at most 0.012.
Values may be sent and summed in bfloat16 or wider, within the bound.
No kernel may reach another device: no remote copies, remote signals or barrier semaphores. Data moves between devices by JAX's collectives and lax.ppermute only.
A program may use at most 128 MiB of HBM per device.

```python
import jax
import jax.numpy as jnp
from jax import lax

CHAIN_LENGTH = 1024
HOMOLOG_COUNT = 256
HOMOLOG_FEATURES = 256
CZ = 128
ATTENTION_HEADS = 8
SIDE_FEATURES = 32
HEAD_CHANNELS = 32


def touch_ends(result, own_key, smallest, largest):
    index_at = [jax.random.randint(jax.random.fold_in(own_key, axis), (), 0, length) for axis, length in enumerate(result.shape)]
    widest = result.shape.index(max(result.shape))
    neighbour = index_at[:widest] + [(index_at[widest] + 1) % result.shape[widest]] + index_at[widest + 1:]
    return result.at[tuple(index_at)].set(smallest).at[tuple(neighbour)].set(largest)


def level_of(stream_key, dims, pieces, least, high):
    def one(dim, parts):
        heights = jax.random.uniform(jax.random.fold_in(jax.random.fold_in(stream_key, 6), dim), (parts,), jnp.float32, least / len(pieces), high / len(pieces))
        return jnp.repeat(jnp.exp(heights), dims[dim] // parts).reshape((-1,) + (1,) * (len(dims) - dim - 1))

    level = one(*pieces[0])
    for cut in pieces[1:]:
        level = level * one(*cut)
    return level


def normal_values(key, shape, scale, reach, cuts=(), dtype=jnp.bfloat16):
    gain = level_of(key, shape, cuts, -0.22, 0.18) if cuts else 1.0
    values = jax.random.normal(key, shape, jnp.float32) * scale * gain
    return jnp.minimum(jnp.maximum(values, -reach), reach).astype(dtype)


def setup_inputs(seed: int = 0) -> dict:
    streams_of = jax.random.split(jax.random.key(seed), 13)
    homolog_stack = normal_values(streams_of[0], (HOMOLOG_COUNT, CHAIN_LENGTH, HOMOLOG_FEATURES), 1.0, 6.0, ((0, 32), (1, 8)))
    couple_tensor = normal_values(streams_of[1], (CHAIN_LENGTH, CHAIN_LENGTH, CZ), 1.0, 6.0, ((0, 32), (1, 8)))
    amino_occupancy = touch_ends((jax.random.randint(streams_of[2], (CHAIN_LENGTH,), 0, 8) < 7).astype(jnp.int32), jax.random.fold_in(streams_of[2], 1), 0, 1)
    homolog_occupancy = touch_ends((jax.random.randint(streams_of[3], (HOMOLOG_COUNT, CHAIN_LENGTH), 0, 4) < 3).astype(jnp.int32), jax.random.fold_in(streams_of[3], 1), 0, 1)
    focus_entry_coefficients = normal_values(streams_of[4], (HOMOLOG_FEATURES, 4 * HOMOLOG_FEATURES), HOMOLOG_FEATURES ** -0.5, 0.375)
    couple_offset_coefficients = normal_values(streams_of[5], (CZ, ATTENTION_HEADS), CZ ** -0.5, 0.5)
    focus_exit_coefficients = normal_values(streams_of[6], (HOMOLOG_FEATURES, HOMOLOG_FEATURES), HOMOLOG_FEATURES ** -0.5, 0.375)
    tensor_entry_coefficients = normal_values(streams_of[7], (HOMOLOG_FEATURES, 2 * SIDE_FEATURES), HOMOLOG_FEATURES ** -0.5, 0.375)
    tensor_exit_coefficients = normal_values(streams_of[8], (SIDE_FEATURES * SIDE_FEATURES, CZ), SIDE_FEATURES ** -0.5, 1.0)
    trio_entry_coefficients = normal_values(streams_of[9], (CZ, 4 * CZ), CZ ** -0.5, 0.5)
    trio_exit_switch = normal_values(streams_of[10], (CZ, CZ), CZ ** -0.5, 0.5)
    trio_exit_coefficients = normal_values(streams_of[11], (CZ, CZ), CZ ** -0.5, 0.5)
    return dict(homolog_stack=homolog_stack, couple_tensor=couple_tensor, amino_occupancy=amino_occupancy, homolog_occupancy=homolog_occupancy, focus_entry_coefficients=focus_entry_coefficients, couple_offset_coefficients=couple_offset_coefficients, focus_exit_coefficients=focus_exit_coefficients, tensor_entry_coefficients=tensor_entry_coefficients, tensor_exit_coefficients=tensor_exit_coefficients, trio_entry_coefficients=trio_entry_coefficients, trio_exit_switch=trio_exit_switch, trio_exit_coefficients=trio_exit_coefficients)


norm_epsilon = 1e-05
masked_logit = 1000000000.0

def standardize_features(values, axis=-1):
    values = values.astype(jnp.float32)
    average = lax.optimization_barrier(jnp.mean(values, axis=axis, keepdims=True))
    centered = values - average
    spread = lax.optimization_barrier(jnp.mean(centered * centered, axis=axis, keepdims=True))
    return centered * lax.rsqrt(spread + norm_epsilon)

def reference(homolog_stack, couple_tensor, amino_occupancy, homolog_occupancy, focus_entry_coefficients, couple_offset_coefficients, focus_exit_coefficients, tensor_entry_coefficients, tensor_exit_coefficients, trio_entry_coefficients, trio_exit_switch, trio_exit_coefficients):
    live_mask = amino_occupancy.astype(jnp.float32)
    homolog_standardized = standardize_features(homolog_stack).astype(jnp.bfloat16)
    combined_linear_map = jnp.dot(homolog_standardized.reshape(-1, HOMOLOG_FEATURES), focus_entry_coefficients, preferred_element_type=jnp.float32)
    combined_linear_map = combined_linear_map.astype(jnp.bfloat16).reshape(HOMOLOG_COUNT, CHAIN_LENGTH, ATTENTION_HEADS, 4 * HEAD_CHANNELS)
    pair_norm = standardize_features(couple_tensor).astype(jnp.bfloat16)
    pair_bias = jnp.einsum('ijc,ch->hij', pair_norm.astype(jnp.float32), couple_offset_coefficients.astype(jnp.float32)).astype(jnp.bfloat16)
    bias_float = pair_bias.astype(jnp.float32)
    key_penalty = (live_mask - 1.0) * masked_logit
    scaling = HEAD_CHANNELS ** (-0.5)

    def row_attention(alignment_row):
        query_rows = alignment_row[:, :, :HEAD_CHANNELS].astype(jnp.float32)
        key_rows = alignment_row[:, :, HEAD_CHANNELS:2 * HEAD_CHANNELS].astype(jnp.float32)
        value_portion = alignment_row[:, :, 2 * HEAD_CHANNELS:3 * HEAD_CHANNELS].astype(jnp.float32)
        gate_values = alignment_row[:, :, 3 * HEAD_CHANNELS:].astype(jnp.float32)
        logits = jnp.einsum('ihd,jhd->hij', query_rows, key_rows) * scaling + bias_float + key_penalty
        weights = jax.nn.softmax(logits, axis=-1).astype(jnp.bfloat16)
        blended = jnp.einsum('hij,jhd->ihd', weights.astype(jnp.float32), value_portion)
        return (blended * jax.nn.sigmoid(gate_values)).astype(jnp.bfloat16)
    focus_outcome = lax.map(row_attention, combined_linear_map)
    homolog_blended_update = jnp.dot(focus_outcome.reshape(-1, HOMOLOG_FEATURES), focus_exit_coefficients, preferred_element_type=jnp.float32)
    homolog_after_update = (homolog_stack.astype(jnp.float32) + homolog_blended_update.reshape(HOMOLOG_COUNT, CHAIN_LENGTH, HOMOLOG_FEATURES)).astype(jnp.bfloat16)
    tensor_standardized = standardize_features(homolog_after_update).astype(jnp.bfloat16)
    source_target_couple = jnp.dot(tensor_standardized.reshape(-1, HOMOLOG_FEATURES), tensor_entry_coefficients, preferred_element_type=jnp.float32)
    source_target_couple = source_target_couple.reshape(HOMOLOG_COUNT, CHAIN_LENGTH, 2 * SIDE_FEATURES)
    row_present = homolog_occupancy.astype(jnp.float32)
    left_projected = (source_target_couple[..., :SIDE_FEATURES] * row_present[..., None]).astype(jnp.bfloat16).reshape(HOMOLOG_COUNT, CHAIN_LENGTH * SIDE_FEATURES)
    right_projected = (source_target_couple[..., SIDE_FEATURES:] * row_present[..., None]).astype(jnp.bfloat16).reshape(HOMOLOG_COUNT, CHAIN_LENGTH * SIDE_FEATURES)
    counts = jnp.dot(row_present.T, row_present, precision=lax.Precision.HIGHEST) + 1.0
    blocked = CHAIN_LENGTH // 16
    weight_grid = tensor_exit_coefficients.astype(jnp.float32).reshape(SIDE_FEATURES, SIDE_FEATURES, CZ)

    def outer_block(offset):
        left_block = lax.dynamic_slice_in_dim(left_projected, offset * SIDE_FEATURES, blocked * SIDE_FEATURES, 1)
        outer_sum = lax.dot_general(left_block, right_projected, (((0,), (0,)), ((), ())), preferred_element_type=jnp.float32)
        outer_sum = outer_sum.astype(jnp.bfloat16).astype(jnp.float32).reshape(blocked, SIDE_FEATURES, CHAIN_LENGTH, SIDE_FEATURES)
        return jnp.einsum('icjd,cdz->ijz', outer_sum, weight_grid)
    offsets = (jnp.arange(16) * blocked).astype(jnp.int32)
    update = lax.map(outer_block, offsets).reshape(CHAIN_LENGTH, CHAIN_LENGTH, CZ)
    pair_mid = couple_tensor.astype(jnp.float32) + update / counts[..., None]
    tri_norm = standardize_features(pair_mid).astype(jnp.bfloat16)
    norm_float = tri_norm.astype(jnp.float32)
    tile_live = live_mask[:, None] * live_mask[None, :]

    def project(index_part):
        columns = trio_entry_coefficients[:, index_part * CZ:(index_part + 1) * CZ].astype(jnp.float32)
        return jnp.einsum('ijc,cz->zij', norm_float, columns)
    left_tri = (jax.nn.sigmoid(project(0)) * project(1) * tile_live).astype(jnp.bfloat16)
    right_tri = (jax.nn.sigmoid(project(2)) * project(3) * tile_live).astype(jnp.bfloat16)
    channel_groups = CZ // 16

    def triangle(operands):
        former, latter = operands
        return jnp.einsum('cik,cjk->cij', former.astype(jnp.float32), latter.astype(jnp.float32)).astype(jnp.bfloat16)
    product = lax.map(triangle, (left_tri.reshape(channel_groups, 16, CHAIN_LENGTH, CHAIN_LENGTH), right_tri.reshape(channel_groups, 16, CHAIN_LENGTH, CHAIN_LENGTH)))
    product = product.reshape(CZ, CHAIN_LENGTH, CHAIN_LENGTH)
    tri_mixed = standardize_features(product, 0).astype(jnp.bfloat16)
    gating_pair = jax.nn.sigmoid(jnp.dot(tri_norm.reshape(-1, CZ), trio_exit_switch, preferred_element_type=jnp.float32)).reshape(CHAIN_LENGTH, CHAIN_LENGTH, CZ)
    triangle_update = jnp.einsum('cij,cz->ijz', tri_mixed.astype(jnp.float32), trio_exit_coefficients.astype(jnp.float32))
    pair_result = (pair_mid + triangle_update * gating_pair).astype(jnp.bfloat16)
    return (homolog_after_update, pair_result)
```

```python
import functools

import jax
import jax.numpy as jnp
from jax import lax
from jax.experimental import pallas as pl
from jax.experimental.pallas import tpu as pltpu
from jax.sharding import Mesh
from jax.sharding import PartitionSpec as P

BRANCH_ROW = ("branch", "row_0", "row_1")
PLANES = ("branch", "row_0")
CHIPS = ("branch", "row_0", "chan")
SWAP = ((0, 1), (1, 0))
EPSILON = 1e-05
MASKED = 1000000000.0
LOG2E = 1.4426950408889634
BF16 = jnp.bfloat16
F32 = jnp.float32
VMEM_LIMIT = 60 * 1024 * 1024


def params(*semantics):
    return pltpu.CompilerParams(
        dimension_semantics=semantics or ("arbitrary",), vmem_limit_bytes=VMEM_LIMIT
    )


def dot(a, b, dims):
    return lax.dot_general(a, b, ((dims[:1], dims[1:]), ((), ())), preferred_element_type=F32)


def standardize(values, axis):
    values = values.astype(F32)
    centered = values - jnp.mean(values, axis=axis, keepdims=True)
    spread = jnp.mean(centered * centered, axis=axis, keepdims=True)
    return centered * lax.rsqrt(spread + EPSILON)


def sigmoid(x):
    return 1.0 / (1.0 + jnp.exp(-x))


def whole(shape):
    return pl.BlockSpec(shape, lambda *_: (0,) * len(shape))


def project_kernel(heads, width, x_ref, w_ref, qkv_ref, gate_ref):
    normed = standardize(x_ref[0], -1).astype(BF16)
    packed = dot(w_ref[...], normed, (1, 1))
    for h in range(heads):
        base = h * 4 * width
        qkv_ref[h, 0] = packed[base : base + 3 * width].astype(BF16)
        gate_ref[0, h * width : (h + 1) * width] = packed[
            base + 3 * width : base + 4 * width
        ].astype(BF16)


def project_msa(stack, weights, heads):
    entries, residues, features = stack.shape
    width = features // heads
    return pl.pallas_call(
        functools.partial(project_kernel, heads, width),
        grid=(entries,),
        in_specs=[
            pl.BlockSpec((1, residues, features), lambda s: (s, 0, 0)),
            whole((4 * features, features)),
        ],
        out_specs=[
            pl.BlockSpec((heads, 1, 3 * width, residues), lambda s: (0, s, 0, 0)),
            pl.BlockSpec((1, features, residues), lambda s: (s, 0, 0)),
        ],
        out_shape=[
            jax.ShapeDtypeStruct((heads, entries, 3 * width, residues), BF16),
            jax.ShapeDtypeStruct((entries, features, residues), BF16),
        ],
        compiler_params=params(),
        name="project_msa",
    )(stack, weights.T)


def attend_kernel(width, me_ref, qkv_ref, mine_ref, other_ref, pen_ref, out_ref, bias_ref):
    block = pl.program_id(0)
    columns, entries = qkv_ref.shape[0], qkv_ref.shape[1]
    lanes = qkv_ref.shape[3]
    tile = mine_ref.shape[2]
    first = me_ref[0] == 0
    for plane in range(mine_ref.shape[0]):
        for j in range(columns):
            a = mine_ref[plane, j].astype(F32)
            b = other_ref[plane, j].astype(F32)
            pen = pen_ref[:, j * lanes : (j + 1) * lanes]
            row = plane * 2 * tile
            at = slice(j * lanes, (j + 1) * lanes)
            bias_ref[row : row + tile, at] = (jnp.where(first, a, b) + pen) * LOG2E
            bias_ref[row + tile : row + 2 * tile, at] = (jnp.where(first, b, a) + pen) * LOG2E
    scale = width ** (-0.5) * LOG2E
    ones = jnp.ones((8, columns * lanes), BF16)
    for s in range(entries):
        query = qkv_ref[block, s, 0:width]
        keys = jnp.concatenate([qkv_ref[j, s, width : 2 * width] for j in range(columns)], axis=1)
        values = jnp.concatenate(
            [qkv_ref[j, s, 2 * width : 3 * width] for j in range(columns)], axis=1
        )
        logits = dot(query, keys, (0, 0)) * scale + bias_ref[...]
        top = jnp.max(logits, axis=1, keepdims=True)
        weights = jnp.exp2(logits - top).astype(BF16)
        blended = dot(jnp.concatenate([values, ones], axis=0), weights, (1, 1))
        out_ref[0, s] = (blended[:width] * (1.0 / blended[width : width + 1])).astype(BF16)


def attend(me, qkv, mine, other, pen, width):
    columns, entries, _, lanes = qkv.shape
    planes, _, tile, _ = mine.shape
    per = lanes // (2 * tile)
    bias_spec = pl.BlockSpec((per, columns, tile, lanes), lambda b, me: (b, 0, 0, 0))
    return pl.pallas_call(
        functools.partial(attend_kernel, width),
        grid_spec=pltpu.PrefetchScalarGridSpec(
            num_scalar_prefetch=1,
            grid=(columns,),
            in_specs=[whole(qkv.shape), bias_spec, bias_spec, whole(pen.shape)],
            out_specs=pl.BlockSpec((1, entries, width, lanes), lambda b, me: (b, 0, 0, 0)),
            scratch_shapes=[pltpu.VMEM((lanes, columns * lanes), F32)],
        ),
        out_shape=jax.ShapeDtypeStruct((columns, entries, width, lanes), BF16),
        compiler_params=params(),
        name="attend",
    )(me, qkv, mine, other, pen)


def sides_kernel(
    side, att_ref, gate_ref, stack_ref, mask_ref, wo_ref, wl_ref, wr_ref, out_ref, left_ref, right_ref, hold_ref
):
    s = pl.program_id(0)
    residues = stack_ref.shape[1]
    attended = att_ref[...].astype(F32).reshape(-1, residues)
    gated = (attended * sigmoid(gate_ref[0].astype(F32))).astype(BF16)
    updated = (stack_ref[0].astype(F32) + dot(gated, wo_ref[...], (0, 0))).astype(BF16)
    out_ref[0] = updated
    normed = standardize(updated, -1).astype(BF16)
    mask = mask_ref[0]
    right = dot(wr_ref[...], normed, (1, 1)) * mask
    hold_ref[pl.ds(s, side, stride=8), :] = right
    hold_ref[pl.ds(side * 8 + s, 1), :] = mask
    group = 128 // side
    spread = dot(normed, wl_ref[...], (1, 0))
    rows = lax.broadcasted_iota(jnp.int32, spread.shape, 0)
    lanes = lax.broadcasted_iota(jnp.int32, spread.shape, 1)
    spread = jnp.where(rows % group == lanes // side, spread, 0.0).astype(BF16)
    to = lax.broadcasted_iota(jnp.int32, (residues // group, residues), 0)
    of = lax.broadcasted_iota(jnp.int32, (residues // group, residues), 1)
    gather = (jnp.where(of // group == to, 1.0, 0.0) * mask).astype(BF16)
    left_ref[0, 0 : residues // group] = dot(gather, spread, (1, 0)).astype(BF16)
    tail = lax.broadcasted_iota(jnp.int32, (16, residues), 0)
    left_ref[0, residues // group :] = jnp.where(tail == 0, mask, 0.0).astype(BF16)

    @pl.when(s == pl.num_programs(0) - 1)
    def _():
        right_ref[...] = hold_ref[...].astype(BF16)


def sides(attended, gate, stack, mask, w_out, w_sides):
    entries, residues, features = stack.shape
    heads, _, width, _ = attended.shape
    side = w_sides.shape[1] // 2
    group = 128 // side
    rows = residues // group + 16
    return pl.pallas_call(
        functools.partial(sides_kernel, side),
        grid=(entries,),
        in_specs=[
            pl.BlockSpec((heads, 1, width, residues), lambda s: (0, s, 0, 0)),
            pl.BlockSpec((1, features, residues), lambda s: (s, 0, 0)),
            pl.BlockSpec((1, residues, features), lambda s: (s, 0, 0)),
            pl.BlockSpec((1, 1, residues), lambda s: (s, 0, 0)),
            whole(w_out.shape),
            whole((features, 128)),
            whole((side, features)),
        ],
        out_specs=[
            pl.BlockSpec((1, residues, features), lambda s: (s, 0, 0)),
            pl.BlockSpec((1, rows, 128), lambda s: (s, 0, 0)),
            whole(((side + 1) * 8, residues)),
        ],
        out_shape=[
            jax.ShapeDtypeStruct(stack.shape, BF16),
            jax.ShapeDtypeStruct((entries, rows, 128), BF16),
            jax.ShapeDtypeStruct(((side + 1) * 8, residues), BF16),
        ],
        scratch_shapes=[pltpu.VMEM(((side + 1) * 8, residues), F32)],
        compiler_params=params(),
        name="sides",
    )(
        attended,
        gate,
        stack,
        mask[:, None, :].astype(F32),
        w_out,
        jnp.tile(w_sides[:, :side], (1, group)),
        w_sides[:, side:].T,
    )


def outer_kernel(
    side, at_ref, left_ref, lmask_ref, right_ref, rmask_ref, couple_ref, live_ref, we_ref, wt_ref,
    mid_ref, l_ref, r_ref, x_ref, count_ref,
):
    step = pl.program_id(0)
    rows, lanes = couple_ref.shape[0], couple_ref.shape[1]
    channels = couple_ref.shape[2]

    @pl.when(step == 0)
    def _():
        count_ref[...] = 1.0 / (dot(lmask_ref[...], rmask_ref[...], (0, 0)) + 1.0)

    wide = 8 * lanes
    for chunk in range(side * lanes // wide):
        outer = dot(
            left_ref[0], right_ref[:, chunk * wide : (chunk + 1) * wide], (0, 0)
        ).astype(BF16)
        for k in range(8):
            d = chunk * 8 + k
            for i in range(rows):
                x_ref[d * side : (d + 1) * side, i * lanes : (i + 1) * lanes] = outer[
                    i * side : (i + 1) * side, k * lanes : (k + 1) * lanes
                ]
    update = dot(we_ref[...], x_ref[...], (1, 0))
    normed = []
    for i in range(rows):
        over = count_ref[pl.ds(at_ref[0] * 32 + step * rows + i, 1), :]
        mid = couple_ref[i].astype(F32).T + update[:, i * lanes : (i + 1) * lanes] * over
        mid_ref[i] = mid
        normed.append(standardize(mid, 0).astype(BF16))
    normed = jnp.concatenate(normed, axis=1)
    for part, ref in ((0, l_ref), (2, r_ref)):
        gate = dot(wt_ref[part * channels : (part + 1) * channels], normed, (1, 0))
        value = dot(wt_ref[(part + 1) * channels : (part + 2) * channels], normed, (1, 0))
        both = sigmoid(gate) * value
        for i in range(rows):
            live = live_ref[pl.ds(step * rows + i, 1), :]
            ref[i] = (both[:, i * lanes : (i + 1) * lanes] * live).astype(BF16)


def outer(at, left, lmask, right, rmask, couple, live, w_exit, w_tri):
    steps, entries, _ = left.shape
    pair_rows, lanes, channels = couple.shape
    rows = pair_rows // steps
    side = right.shape[1] // lanes
    tile = pl.BlockSpec((rows, channels, lanes), lambda t, at: (t, 0, 0))
    w_exit = w_exit.reshape(side, side, channels).transpose(2, 1, 0).reshape(channels, side * side)
    return pl.pallas_call(
        functools.partial(outer_kernel, side),
        grid_spec=pltpu.PrefetchScalarGridSpec(
            num_scalar_prefetch=1,
            grid=(steps,),
            in_specs=[
                pl.BlockSpec((1, entries, 128), lambda t, at: (t, 0, 0)),
                whole(lmask.shape),
                whole(right.shape),
                whole(rmask.shape),
                pl.BlockSpec((rows, lanes, channels), lambda t, at: (t, 0, 0)),
                whole(live.shape),
                whole(w_exit.shape),
                whole((4 * channels, channels)),
            ],
            out_specs=[tile, tile, tile],
            scratch_shapes=[
                pltpu.VMEM((side * side, rows * lanes), BF16),
                pltpu.VMEM((128, lanes), F32),
            ],
        ),
        out_shape=[
            jax.ShapeDtypeStruct((pair_rows, channels, lanes), F32),
            jax.ShapeDtypeStruct((pair_rows, channels, lanes), BF16),
            jax.ShapeDtypeStruct((pair_rows, channels, lanes), BF16),
        ],
        compiler_params=params(),
        name="outer",
    )(at, left, lmask, right, rmask, couple, live, w_exit, w_tri.T)


def triangle_kernel(me_ref, l_ref, mine_ref, other_ref, out_ref):
    planes, columns, tile, lanes = l_ref.shape
    first = me_ref[0] == 0
    joined = lambda ref, p: jnp.concatenate([ref[p, k] for k in range(columns)], axis=1)
    rights = []
    for p in range(mine_ref.shape[0]):
        a, b = joined(mine_ref, p), joined(other_ref, p)
        rights += [jnp.where(first, a, b), jnp.where(first, b, a)]
    right = jnp.concatenate(rights, axis=0)
    per = lanes // (2 * tile)
    for p in range(0, planes, 4):
        left = jnp.concatenate([joined(l_ref, p + q) for q in range(4)], axis=0)
        product = dot(left, right, (1, 1)).astype(BF16)
        for q in range(4):
            for n in range(mine_ref.shape[0] // per):
                out_ref[p + q, n] = product[
                    q * tile : (q + 1) * tile, n * lanes : (n + 1) * lanes
                ]


def triangle(me, left, mine, other):
    planes, columns, tile, lanes = left.shape
    per = lanes // (2 * tile)
    take = 2
    spec = pl.BlockSpec((per * take, columns, tile, lanes), lambda n, me: (n, 0, 0, 0))
    return pl.pallas_call(
        triangle_kernel,
        grid_spec=pltpu.PrefetchScalarGridSpec(
            num_scalar_prefetch=1,
            grid=(columns // take,),
            in_specs=[whole(left.shape), spec, spec],
            out_specs=pl.BlockSpec((planes, take, tile, lanes), lambda n, me: (0, n, 0, 0)),
        ),
        out_shape=jax.ShapeDtypeStruct(left.shape, BF16),
        compiler_params=params(),
        name="triangle",
    )(me, left, mine, other)


def finish_kernel(prod_ref, mid_ref, wo_ref, ws_ref, out_ref, mixed_ref):
    step = pl.program_id(0)
    channels, pair_rows, lanes = prod_ref.shape
    rows = mid_ref.shape[0]

    @pl.when(step == 0)
    def _():
        total = jnp.zeros((pair_rows, lanes), F32)
        for c in range(channels):
            total = total + prod_ref[c].astype(F32)
        mean = total / channels
        spread = jnp.zeros((pair_rows, lanes), F32)
        for c in range(channels):
            centered = prod_ref[c].astype(F32) - mean
            spread = spread + centered * centered
        inverse = lax.rsqrt(spread / channels + EPSILON)
        for c in range(channels):
            mixed_ref[c * pair_rows : (c + 1) * pair_rows, :] = (
                prod_ref[c].astype(F32) - mean
            ) * inverse

    mixed, normed = [], []
    for i in range(rows):
        mixed.append(
            mixed_ref[pl.ds(step * rows + i, channels, stride=pair_rows), :].astype(BF16)
        )
        normed.append(standardize(mid_ref[i], 0).astype(BF16))
    update = dot(wo_ref[...], jnp.concatenate(mixed, axis=1), (1, 0))
    gate = sigmoid(dot(ws_ref[...], jnp.concatenate(normed, axis=1), (1, 0)))
    update = update * gate
    for i in range(rows):
        result = mid_ref[i] + update[:, i * lanes : (i + 1) * lanes]
        out_ref[i] = result.T.astype(BF16)


def finish(product, mid, w_out, w_switch):
    channels, pair_rows, lanes = product.shape
    rows = 4
    return pl.pallas_call(
        finish_kernel,
        grid=(pair_rows // rows,),
        in_specs=[
            whole(product.shape),
            pl.BlockSpec((rows, channels, lanes), lambda t: (t, 0, 0)),
            whole(w_out.shape),
            whole(w_switch.shape),
        ],
        out_specs=pl.BlockSpec((rows, lanes, channels), lambda t: (t, 0, 0)),
        out_shape=jax.ShapeDtypeStruct((pair_rows, lanes, channels), BF16),
        scratch_shapes=[pltpu.VMEM((channels * pair_rows, lanes), F32)],
        compiler_params=params(),
        name="finish",
    )(product, mid, w_out.T, w_switch.T)


def swap(x):
    return lax.ppermute(x, "row_1", SWAP)


def exchange(x, axes):
    return lax.all_to_all(x, axes, 0, 0, tiled=True)


def repeated(x, n):
    return jnp.broadcast_to(x[None], (n, *x.shape))


def shards(
    homolog_stack,
    couple_tensor,
    amino_occupancy,
    homolog_occupancy,
    focus_entry_coefficients,
    couple_offset_coefficients,
    focus_exit_coefficients,
    tensor_entry_coefficients,
    tensor_exit_coefficients,
    trio_entry_coefficients,
    trio_exit_switch,
    trio_exit_coefficients,
):
    entries, residues, features = homolog_stack.shape
    pair_rows, pair_cols, pair_width = couple_tensor.shape
    heads = couple_offset_coefficients.shape[1]
    width = features // heads
    side = tensor_entry_coefficients.shape[1] // 2
    planes = lax.axis_size("branch") * lax.axis_size("row_0")
    chan = lax.axis_size("chan")
    core = lax.axis_index("row_1").astype(jnp.int32)
    row = lax.axis_index(BRANCH_ROW).astype(jnp.int32)
    me = core.reshape(1)
    live = amino_occupancy.astype(F32)
    live_rows = lax.dynamic_slice_in_dim(live, row * pair_rows, pair_rows)
    live_cols = lax.dynamic_slice_in_dim(live, lax.axis_index("chan") * pair_cols, pair_cols)
    penalty = ((live - 1.0) * MASKED)[None, :]

    pair_norm = standardize(couple_tensor, -1).astype(BF16)
    bias = jnp.einsum(
        "ijc,ch->hij", pair_norm, couple_offset_coefficients, preferred_element_type=F32
    ).astype(BF16)
    bias = exchange(bias, "chan")
    bias = exchange(repeated(bias, planes), PLANES)
    bias_other = swap(bias)

    qkv, gate = project_msa(homolog_stack, focus_entry_coefficients, heads)
    qkv = exchange(qkv, "chan")
    attended = attend(me, qkv, bias, bias_other, penalty, width)
    attended = exchange(attended, "chan")

    homolog_after_update, left, right = sides(
        attended,
        gate,
        homolog_stack,
        homolog_occupancy,
        focus_exit_coefficients,
        tensor_entry_coefficients,
    )
    left = exchange(left, "chan")
    packed_rows = residues * side // 128
    per_plane = left.shape[0] * packed_rows // planes
    parts = jnp.concatenate(
        [
            repeated(right, planes),
            left[:, :packed_rows].reshape(planes, per_plane, 128),
            jnp.repeat(left[:, packed_rows : packed_rows + 8], planes // chan, axis=0),
        ],
        axis=1,
    )
    mine = exchange(parts, PLANES)
    other = swap(mine)
    both = jnp.stack([mine, other]).reshape(2 * planes, *mine.shape[1:])
    sources = 2 * planes
    wide = side * 8
    right_all = both[:, :wide].reshape(sources, side, 8, pair_cols)
    right_all = right_all.transpose(0, 2, 1, 3).reshape(sources * 8, side * pair_cols)
    right_mask = both[:, wide : wide + 8].reshape(sources * 8, pair_cols)
    tail = both[:, wide + 8 :]
    mine_left = lax.dynamic_slice_in_dim(tail, core * (per_plane // 2), per_plane // 2, 1)
    left = jnp.concatenate([mine_left, tail[:, per_plane : per_plane + 1]], axis=1)
    left = exchange(repeated(left.transpose(1, 0, 2), chan), "chan")
    left = left.transpose(1, 2, 0, 3).reshape(left.shape[1], sources * chan, 128)
    steps = per_plane // 2
    mid, left_tri, right_tri = outer(
        (row % 4).reshape(1),
        left[:steps],
        left[steps],
        right_all,
        right_mask,
        couple_tensor,
        live_rows[:, None] * live_cols[None, :],
        tensor_exit_coefficients,
        trio_entry_coefficients,
    )
    operands = jnp.stack([left_tri, right_tri]).transpose(2, 0, 1, 3)
    operands = exchange(operands, CHIPS)
    grid = (planes, chan, pair_rows, pair_cols)
    left_tri, right_tri = operands[:, 0].reshape(grid), operands[:, 1].reshape(grid)
    product = triangle(me, left_tri, right_tri, swap(right_tri))
    product = exchange(product.reshape(pair_width, pair_rows, pair_cols), CHIPS)
    pair_result = finish(product, mid, trio_exit_coefficients, trio_exit_switch)
    return (homolog_after_update, pair_result)


def solution(mesh):
    torus = Mesh(
        mesh.devices.reshape(mesh.shape["branch"], 8, 2, mesh.shape["chan"]),
        ("branch", "row_0", "row_1", "chan"),
    )
    return jax.shard_map(
        shards,
        mesh=torus,
        in_specs=(
            P(BRANCH_ROW, "chan", None),
            P(BRANCH_ROW, "chan", None),
            P(),
            P(BRANCH_ROW, "chan"),
            *(P() for _ in range(8)),
        ),
        out_specs=(P(BRANCH_ROW, "chan", None), P(BRANCH_ROW, "chan", None)),
        check_vma=False,
    )
```

```python
import functools

import jax
import jax.numpy as jnp
from jax import lax
from jax.experimental import pallas as pl
from jax.experimental.pallas import tpu as pltpu
from jax.sharding import Mesh
from jax.sharding import PartitionSpec as P


BRANCH_ROW = ("branch", "row_0", "row_1")
CHIPS = ("branch", "row_0", "chan")
SWAP = ((0, 1), (1, 0))
EPSILON = 1e-05
MASKED = 1000000000.0
LOG2E = 1.4426950408889634
BF16 = jnp.bfloat16
F32 = jnp.float32
VMEM_LIMIT = 60 * 1024 * 1024


def params(*semantics):
    return pltpu.CompilerParams(
        dimension_semantics=semantics or ("arbitrary",), vmem_limit_bytes=VMEM_LIMIT
    )


def dot(a, b, dims):
    return lax.dot_general(a, b, ((dims[:1], dims[1:]), ((), ())), preferred_element_type=F32)


def standardize(values, axis):
    values = values.astype(F32)
    centered = values - jnp.mean(values, axis=axis, keepdims=True)
    spread = jnp.mean(centered * centered, axis=axis, keepdims=True)
    return centered * lax.rsqrt(spread + EPSILON)


def sigmoid(x):
    return 1.0 / (1.0 + jnp.exp(-x))


def whole(shape):
    return pl.BlockSpec(shape, lambda *_: (0,) * len(shape))


def project_kernel(heads, width, x_ref, w_ref, qkv_ref, gate_ref):
    normed = standardize(x_ref[0], -1).astype(BF16)
    packed = dot(w_ref[...], normed, (1, 1))
    for h in range(heads):
        base = h * 4 * width
        qkv_ref[h, 0] = packed[base : base + 3 * width].astype(BF16)
        gate_ref[0, h * width : (h + 1) * width] = packed[
            base + 3 * width : base + 4 * width
        ].astype(BF16)


def project_msa(stack, weights, heads):
    entries, residues, features = stack.shape
    width = features // heads
    return pl.pallas_call(
        functools.partial(project_kernel, heads, width),
        grid=(entries,),
        in_specs=[
            pl.BlockSpec((1, residues, features), lambda s: (s, 0, 0)),
            whole((4 * features, features)),
        ],
        out_specs=[
            pl.BlockSpec((heads, 1, 3 * width, residues), lambda s: (0, s, 0, 0)),
            pl.BlockSpec((1, features, residues), lambda s: (s, 0, 0)),
        ],
        out_shape=[
            jax.ShapeDtypeStruct((heads, entries, 3 * width, residues), BF16),
            jax.ShapeDtypeStruct((entries, features, residues), BF16),
        ],
        compiler_params=params(),
        name="project_msa",
    )(stack, weights.T)


def attend_kernel(width, at_ref, qkv_ref, mine_ref, other_ref, pen_ref, out_ref, bias_ref):
    block = pl.program_id(0)
    columns, entries = qkv_ref.shape[0], qkv_ref.shape[1]
    lanes = qkv_ref.shape[3]
    length, _, _, tile, _ = mine_ref.shape
    first = at_ref[0] == 0
    for q in range(lanes // (2 * tile)):
        plane = block * (lanes // (2 * tile)) + q
        place = ring_place((plane + 2 * length - at_ref[2]) % length, length)
        side = jnp.bitwise_xor(plane // length, at_ref[1])
        for j in range(columns):
            a = mine_ref[place, side, j].astype(F32)
            b = other_ref[place, side, j].astype(F32)
            pen = pen_ref[:, j * lanes : (j + 1) * lanes]
            row = q * 2 * tile
            at = slice(j * lanes, (j + 1) * lanes)
            bias_ref[row : row + tile, at] = (jnp.where(first, a, b) + pen) * LOG2E
            bias_ref[row + tile : row + 2 * tile, at] = (jnp.where(first, b, a) + pen) * LOG2E
    scale = width ** (-0.5) * LOG2E
    ones = jnp.ones((8, columns * lanes), BF16)
    for s in range(entries):
        query = qkv_ref[block, s, 0:width]
        keys = jnp.concatenate([qkv_ref[j, s, width : 2 * width] for j in range(columns)], axis=1)
        values = jnp.concatenate(
            [qkv_ref[j, s, 2 * width : 3 * width] for j in range(columns)], axis=1
        )
        logits = dot(query, keys, (0, 0)) * scale + bias_ref[...]
        top = jnp.max(logits, axis=1, keepdims=True)
        weights = jnp.exp2(logits - top).astype(BF16)
        blended = dot(jnp.concatenate([values, ones], axis=0), weights, (1, 1))
        out_ref[0, s] = (blended[:width] * (1.0 / blended[width : width + 1])).astype(BF16)


def attend(at, qkv, mine, other, pen, width):
    columns, entries, _, lanes = qkv.shape
    return pl.pallas_call(
        functools.partial(attend_kernel, width),
        grid_spec=pltpu.PrefetchScalarGridSpec(
            num_scalar_prefetch=1,
            grid=(columns,),
            in_specs=[whole(qkv.shape), whole(mine.shape), whole(other.shape), whole(pen.shape)],
            out_specs=pl.BlockSpec((1, entries, width, lanes), lambda b, at: (b, 0, 0, 0)),
            scratch_shapes=[pltpu.VMEM((lanes, columns * lanes), F32)],
        ),
        out_shape=jax.ShapeDtypeStruct((columns, entries, width, lanes), BF16),
        compiler_params=params(),
        name="attend",
    )(at, qkv, mine, other, pen)


def sides_kernel(
    side, att_ref, gate_ref, stack_ref, mask_ref, wo_ref, wl_ref, wr_ref, out_ref, left_ref, right_ref, hold_ref
):
    s = pl.program_id(0)
    residues = stack_ref.shape[1]
    attended = att_ref[...].astype(F32).reshape(-1, residues)
    gated = (attended * sigmoid(gate_ref[0].astype(F32))).astype(BF16)
    updated = (stack_ref[0].astype(F32) + dot(gated, wo_ref[...], (0, 0))).astype(BF16)
    out_ref[0] = updated
    normed = standardize(updated, -1).astype(BF16)
    mask = mask_ref[0]
    right = dot(wr_ref[...], normed, (1, 1)) * mask
    hold_ref[pl.ds(s, side, stride=8), :] = right
    hold_ref[pl.ds(side * 8 + s, 1), :] = mask
    group = 128 // side
    spread = dot(normed, wl_ref[...], (1, 0))
    rows = lax.broadcasted_iota(jnp.int32, spread.shape, 0)
    lanes = lax.broadcasted_iota(jnp.int32, spread.shape, 1)
    spread = jnp.where(rows % group == lanes // side, spread, 0.0).astype(BF16)
    to = lax.broadcasted_iota(jnp.int32, (residues // group, residues), 0)
    of = lax.broadcasted_iota(jnp.int32, (residues // group, residues), 1)
    gather = (jnp.where(of // group == to, 1.0, 0.0) * mask).astype(BF16)
    left_ref[0, 0 : residues // group] = dot(gather, spread, (1, 0)).astype(BF16)
    tail = lax.broadcasted_iota(jnp.int32, (16, residues), 0)
    left_ref[0, residues // group :] = jnp.where(tail == 0, mask, 0.0).astype(BF16)

    @pl.when(s == pl.num_programs(0) - 1)
    def _():
        right_ref[...] = hold_ref[...].astype(BF16)


def sides(attended, gate, stack, mask, w_out, w_sides):
    entries, residues, features = stack.shape
    heads, _, width, _ = attended.shape
    side = w_sides.shape[1] // 2
    group = 128 // side
    rows = residues // group + 16
    return pl.pallas_call(
        functools.partial(sides_kernel, side),
        grid=(entries,),
        in_specs=[
            pl.BlockSpec((heads, 1, width, residues), lambda s: (0, s, 0, 0)),
            pl.BlockSpec((1, features, residues), lambda s: (s, 0, 0)),
            pl.BlockSpec((1, residues, features), lambda s: (s, 0, 0)),
            pl.BlockSpec((1, 1, residues), lambda s: (s, 0, 0)),
            whole(w_out.shape),
            whole((features, 128)),
            whole((side, features)),
        ],
        out_specs=[
            pl.BlockSpec((1, residues, features), lambda s: (s, 0, 0)),
            pl.BlockSpec((1, rows, 128), lambda s: (s, 0, 0)),
            whole(((side + 1) * 8, residues)),
        ],
        out_shape=[
            jax.ShapeDtypeStruct(stack.shape, BF16),
            jax.ShapeDtypeStruct((entries, rows, 128), BF16),
            jax.ShapeDtypeStruct(((side + 1) * 8, residues), BF16),
        ],
        scratch_shapes=[pltpu.VMEM(((side + 1) * 8, residues), F32)],
        compiler_params=params(),
        name="sides",
    )(
        attended,
        gate,
        stack,
        mask[:, None, :].astype(F32),
        w_out,
        jnp.tile(w_sides[:, :side], (1, group)),
        w_sides[:, side:].T,
    )


def outer_kernel(
    side, at_ref, left_ref, lmask_ref, mine_ref, other_ref, couple_ref, live_ref, we_ref, wt_ref,
    mid_ref, l_ref, r_ref, right_ref, rmask_ref, x_ref, count_ref,
):
    step = pl.program_id(0)
    rows, lanes = couple_ref.shape[0], couple_ref.shape[1]
    channels = couple_ref.shape[2]

    @pl.when(step == 0)
    def _():
        length, branches = mine_ref.shape[0], mine_ref.shape[1]
        for branch in range(branches):
            for z in range(length):
                place = ring_place((z + length - at_ref[2]) % length, length)
                which = jnp.bitwise_xor(branch, at_ref[1])
                row = (branch * length + z) * 16
                for d in range(side + 1):
                    pair = [ref[place, which, d * 8 : (d + 1) * 8] for ref in (mine_ref, other_ref)]
                    pair = jnp.concatenate(pair, axis=0)
                    if d < side:
                        right_ref[row : row + 16, d * lanes : (d + 1) * lanes] = pair
                    else:
                        rmask_ref[row : row + 16, :] = pair
        count_ref[...] = 1.0 / (dot(lmask_ref[...], rmask_ref[...], (0, 0)) + 1.0)

    wide = 8 * lanes
    for chunk in range(side * lanes // wide):
        outer = dot(
            left_ref[0], right_ref[:, chunk * wide : (chunk + 1) * wide], (0, 0)
        ).astype(BF16)
        for k in range(8):
            d = chunk * 8 + k
            for i in range(rows):
                x_ref[d * side : (d + 1) * side, i * lanes : (i + 1) * lanes] = outer[
                    i * side : (i + 1) * side, k * lanes : (k + 1) * lanes
                ]
    update = dot(we_ref[...], x_ref[...], (1, 0))
    normed = []
    for i in range(rows):
        over = count_ref[pl.ds(at_ref[3] * 32 + step * rows + i, 1), :]
        mid = couple_ref[i].astype(F32).T + update[:, i * lanes : (i + 1) * lanes] * over
        mid_ref[i] = mid
        normed.append(standardize(mid, 0).astype(BF16))
    normed = jnp.concatenate(normed, axis=1)
    for part, ref in ((0, l_ref), (2, r_ref)):
        gate = dot(wt_ref[part * channels : (part + 1) * channels], normed, (1, 0))
        value = dot(wt_ref[(part + 1) * channels : (part + 2) * channels], normed, (1, 0))
        both = sigmoid(gate) * value
        for i in range(rows):
            live = live_ref[pl.ds(step * rows + i, 1), :]
            ref[i] = (both[:, i * lanes : (i + 1) * lanes] * live).astype(BF16)


def outer(at, left, lmask, mine, other, couple, live, w_exit, w_tri):
    steps, entries, _ = left.shape
    pair_rows, lanes, channels = couple.shape
    rows = pair_rows // steps
    side = mine.shape[2] // 8 - 1
    tile = pl.BlockSpec((rows, channels, lanes), lambda t, at: (t, 0, 0))
    w_exit = w_exit.reshape(side, side, channels).transpose(2, 1, 0).reshape(channels, side * side)
    return pl.pallas_call(
        functools.partial(outer_kernel, side),
        grid_spec=pltpu.PrefetchScalarGridSpec(
            num_scalar_prefetch=1,
            grid=(steps,),
            in_specs=[
                pl.BlockSpec((1, entries, 128), lambda t, at: (t, 0, 0)),
                whole(lmask.shape),
                whole(mine.shape),
                whole(other.shape),
                pl.BlockSpec((rows, lanes, channels), lambda t, at: (t, 0, 0)),
                whole(live.shape),
                whole(w_exit.shape),
                whole((4 * channels, channels)),
            ],
            out_specs=[tile, tile, tile],
            scratch_shapes=[
                pltpu.VMEM((entries, side * lanes), BF16),
                pltpu.VMEM((entries, lanes), BF16),
                pltpu.VMEM((side * side, rows * lanes), BF16),
                pltpu.VMEM((128, lanes), F32),
            ],
        ),
        out_shape=[
            jax.ShapeDtypeStruct((pair_rows, channels, lanes), F32),
            jax.ShapeDtypeStruct((pair_rows, channels, lanes), BF16),
            jax.ShapeDtypeStruct((pair_rows, channels, lanes), BF16),
        ],
        compiler_params=params(),
        name="outer",
    )(at, left, lmask, mine, other, couple, live, w_exit, w_tri.T)


def triangle_kernel(me_ref, l_ref, mine_ref, other_ref, out_ref):
    planes, columns, tile, lanes = l_ref.shape
    first = me_ref[0] == 0
    joined = lambda ref, p: jnp.concatenate([ref[p, k] for k in range(columns)], axis=1)
    rights = []
    for p in range(mine_ref.shape[0]):
        a, b = joined(mine_ref, p), joined(other_ref, p)
        rights += [jnp.where(first, a, b), jnp.where(first, b, a)]
    right = jnp.concatenate(rights, axis=0)
    per = lanes // (2 * tile)
    for p in range(0, planes, 4):
        left = jnp.concatenate([joined(l_ref, p + q) for q in range(4)], axis=0)
        product = dot(left, right, (1, 1)).astype(BF16)
        for q in range(4):
            for n in range(mine_ref.shape[0] // per):
                out_ref[p + q, n] = product[
                    q * tile : (q + 1) * tile, n * lanes : (n + 1) * lanes
                ]


def triangle(me, left, mine, other):
    planes, columns, tile, lanes = left.shape
    per = lanes // (2 * tile)
    take = 2
    spec = pl.BlockSpec((per * take, columns, tile, lanes), lambda n, me: (n, 0, 0, 0))
    return pl.pallas_call(
        triangle_kernel,
        grid_spec=pltpu.PrefetchScalarGridSpec(
            num_scalar_prefetch=1,
            grid=(columns // take,),
            in_specs=[whole(left.shape), spec, spec],
            out_specs=pl.BlockSpec((planes, take, tile, lanes), lambda n, me: (0, n, 0, 0)),
        ),
        out_shape=jax.ShapeDtypeStruct(left.shape, BF16),
        compiler_params=params(),
        name="triangle",
    )(me, left, mine, other)


def finish_kernel(prod_ref, mid_ref, wo_ref, ws_ref, out_ref, mixed_ref):
    step = pl.program_id(0)
    channels, pair_rows, lanes = prod_ref.shape
    rows = mid_ref.shape[0]

    @pl.when(step == 0)
    def _():
        total = jnp.zeros((pair_rows, lanes), F32)
        for c in range(channels):
            total = total + prod_ref[c].astype(F32)
        mean = total / channels
        spread = jnp.zeros((pair_rows, lanes), F32)
        for c in range(channels):
            centered = prod_ref[c].astype(F32) - mean
            spread = spread + centered * centered
        inverse = lax.rsqrt(spread / channels + EPSILON)
        for c in range(channels):
            mixed_ref[c * pair_rows : (c + 1) * pair_rows, :] = (
                prod_ref[c].astype(F32) - mean
            ) * inverse

    mixed, normed = [], []
    for i in range(rows):
        mixed.append(
            mixed_ref[pl.ds(step * rows + i, channels, stride=pair_rows), :].astype(BF16)
        )
        normed.append(standardize(mid_ref[i], 0).astype(BF16))
    update = dot(wo_ref[...], jnp.concatenate(mixed, axis=1), (1, 0))
    gate = sigmoid(dot(ws_ref[...], jnp.concatenate(normed, axis=1), (1, 0)))
    update = update * gate
    for i in range(rows):
        result = mid_ref[i] + update[:, i * lanes : (i + 1) * lanes]
        out_ref[i] = result.T.astype(BF16)


def finish(product, mid, w_out, w_switch):
    channels, pair_rows, lanes = product.shape
    rows = 4
    return pl.pallas_call(
        finish_kernel,
        grid=(pair_rows // rows,),
        in_specs=[
            whole(product.shape),
            pl.BlockSpec((rows, channels, lanes), lambda t: (t, 0, 0)),
            whole(w_out.shape),
            whole(w_switch.shape),
        ],
        out_specs=pl.BlockSpec((rows, lanes, channels), lambda t: (t, 0, 0)),
        out_shape=jax.ShapeDtypeStruct((pair_rows, lanes, channels), BF16),
        scratch_shapes=[pltpu.VMEM((channels * pair_rows, lanes), F32)],
        compiler_params=params(),
        name="finish",
    )(product, mid, w_out.T, w_switch.T)


def swap(x):
    return lax.ppermute(x, "row_1", SWAP)


def exchange(x, axes):
    return lax.all_to_all(x, axes, 0, 0, tiled=True)


def ring_gather(x):
    n = lax.axis_size("row_0")
    up = tuple((k, (k + 1) % n) for k in range(n))
    down = tuple((k, (k - 1) % n) for k in range(n))
    pair = jnp.stack([x, lax.ppermute(x, "branch", SWAP)])
    places, above, below = [pair], pair, pair
    for _ in range(n // 2 - 1):
        above = lax.ppermute(above, "row_0", up)
        below = lax.ppermute(below, "row_0", down)
        places += [above, below]
    last = [lax.ppermute(above[:1], "row_0", up), lax.ppermute(below[1:], "row_0", down)]
    places.append(jnp.concatenate(last))
    return jnp.stack(places)


def ring_place(ahead, n):
    return jnp.where(ahead <= n // 2, jnp.maximum(2 * ahead - (ahead == n // 2), 0), 2 * (n - ahead) - 1)


def repeated(x, n):
    return jnp.broadcast_to(x[None], (n, *x.shape))


def shards(
    homolog_stack,
    couple_tensor,
    amino_occupancy,
    homolog_occupancy,
    focus_entry_coefficients,
    couple_offset_coefficients,
    focus_exit_coefficients,
    tensor_entry_coefficients,
    tensor_exit_coefficients,
    trio_entry_coefficients,
    trio_exit_switch,
    trio_exit_coefficients,
):
    _, residues, features = homolog_stack.shape
    pair_rows, pair_cols, pair_width = couple_tensor.shape
    heads = couple_offset_coefficients.shape[1]
    width = features // heads
    side = tensor_entry_coefficients.shape[1] // 2
    planes = lax.axis_size("branch") * lax.axis_size("row_0")
    chan = lax.axis_size("chan")
    core = lax.axis_index("row_1").astype(jnp.int32)
    row = lax.axis_index(BRANCH_ROW).astype(jnp.int32)
    place = [core, lax.axis_index("branch"), lax.axis_index("row_0"), row % 4]
    at = jnp.stack([p.astype(jnp.int32) for p in place])
    me = core.reshape(1)
    live = amino_occupancy.astype(F32)
    live_rows = lax.dynamic_slice_in_dim(live, row * pair_rows, pair_rows)
    live_cols = lax.dynamic_slice_in_dim(live, lax.axis_index("chan") * pair_cols, pair_cols)
    penalty = ((live - 1.0) * MASKED)[None, :]

    pair_norm = standardize(couple_tensor, -1).astype(BF16)
    bias = jnp.einsum(
        "ijc,ch->hij", pair_norm, couple_offset_coefficients, preferred_element_type=F32
    ).astype(BF16)
    bias = exchange(bias, "chan")
    bias = ring_gather(bias)
    bias_other = swap(bias)

    qkv, gate = project_msa(homolog_stack, focus_entry_coefficients, heads)
    qkv = exchange(qkv, "chan")
    attended = attend(at, qkv, bias, bias_other, penalty, width)
    attended = exchange(attended, "chan")

    homolog_after_update, left, right = sides(
        attended,
        gate,
        homolog_stack,
        homolog_occupancy,
        focus_exit_coefficients,
        tensor_entry_coefficients,
    )
    right = ring_gather(right)
    right_other = swap(right)
    left = exchange(left, "chan")
    members = 2 * planes
    packed_rows = residues * side // 128
    steps = chan * packed_rows // members
    left = jnp.concatenate(
        [
            left[:, :packed_rows].reshape(members, steps, 128),
            jnp.repeat(left[:, packed_rows : packed_rows + 8], members // chan, axis=0),
        ],
        axis=1,
    )
    left = exchange(left, BRANCH_ROW)
    left = left[:, : steps + 1].reshape(planes, 2, steps + 1, 128)
    left = jnp.where(core == 0, left, left[:, ::-1]).reshape(members, steps + 1, 128)
    left = exchange(repeated(left.transpose(1, 0, 2), chan), "chan")
    left = left.transpose(1, 2, 0, 3).reshape(steps + 1, members * chan, 128)
    mid, left_tri, right_tri = outer(
        at,
        left[:steps],
        left[steps],
        right,
        right_other,
        couple_tensor,
        live_rows[:, None] * live_cols[None, :],
        tensor_exit_coefficients,
        trio_entry_coefficients,
    )
    operands = jnp.stack([left_tri, right_tri]).transpose(2, 0, 1, 3)
    operands = exchange(operands, CHIPS)
    grid = (planes, chan, pair_rows, pair_cols)
    left_tri, right_tri = operands[:, 0].reshape(grid), operands[:, 1].reshape(grid)
    product = triangle(me, left_tri, right_tri, swap(right_tri))
    product = exchange(product.reshape(pair_width, pair_rows, pair_cols), CHIPS)
    pair_result = finish(product, mid, trio_exit_coefficients, trio_exit_switch)
    return (homolog_after_update, pair_result)


def solution(mesh):
    torus = Mesh(
        mesh.devices.reshape(mesh.shape["branch"], 8, 2, mesh.shape["chan"]),
        ("branch", "row_0", "row_1", "chan"),
    )

    return jax.shard_map(
        shards,
        mesh=torus,
        in_specs=(
            P(BRANCH_ROW, "chan", None),
            P(BRANCH_ROW, "chan", None),
            P(),
            P(BRANCH_ROW, "chan"),
            *(P() for _ in range(8)),
        ),
        out_specs=(P(BRANCH_ROW, "chan", None), P(BRANCH_ROW, "chan", None)),
        check_vma=False,
    )
```

```python
import functools

import jax
import jax.numpy as jnp
from jax import lax
from jax.experimental import pallas as pl
from jax.experimental.pallas import tpu as pltpu
from jax.sharding import Mesh
from jax.sharding import PartitionSpec as P


BRANCH_ROW = ("branch", "row_0", "row_1")
CHIPS = ("branch", "row_0", "chan")
SWAP = ((0, 1), (1, 0))
EPSILON = 1e-05
MASKED = 1000000000.0
LOG2E = 1.4426950408889634
BF16 = jnp.bfloat16
F32 = jnp.float32


def params(mebibytes):
    return pltpu.CompilerParams(
        dimension_semantics=("arbitrary",), vmem_limit_bytes=mebibytes * 1024 * 1024
    )


def dot(a, b, dims):
    return lax.dot_general(a, b, ((dims[:1], dims[1:]), ((), ())), preferred_element_type=F32)


def standardize(values, axis):
    values = values.astype(F32)
    centered = values - jnp.mean(values, axis=axis, keepdims=True)
    spread = jnp.mean(centered * centered, axis=axis, keepdims=True)
    return centered * lax.rsqrt(spread + EPSILON)


def sigmoid(x):
    return 1.0 / (1.0 + jnp.exp(-x))


def whole(shape):
    return pl.BlockSpec(shape, lambda *_: (0,) * len(shape))


def project_kernel(heads, width, x_ref, w_ref, qkv_ref, gate_ref):
    entries, residues, features = x_ref.shape
    normed = standardize(x_ref[...].reshape(entries * residues, features), -1).astype(BF16)
    packed = dot(w_ref[...], normed, (1, 1)).astype(BF16)
    for s in range(entries):
        at = slice(s * residues, (s + 1) * residues)
        for h in range(heads):
            base = h * 4 * width
            qkv_ref[h, s] = packed[base : base + 3 * width, at]
            gate_ref[s, h * width : (h + 1) * width] = packed[
                base + 3 * width : base + 4 * width, at
            ]


def project_msa(stack, weights, heads):
    entries, residues, features = stack.shape
    width = features // heads
    take = 2
    return pl.pallas_call(
        functools.partial(project_kernel, heads, width),
        grid=(entries // take,),
        in_specs=[
            pl.BlockSpec((take, residues, features), lambda s: (s, 0, 0)),
            whole((4 * features, features)),
        ],
        out_specs=[
            pl.BlockSpec((heads, take, 3 * width, residues), lambda s: (0, s, 0, 0)),
            pl.BlockSpec((take, features, residues), lambda s: (s, 0, 0)),
        ],
        out_shape=[
            jax.ShapeDtypeStruct((heads, entries, 3 * width, residues), BF16),
            jax.ShapeDtypeStruct((entries, features, residues), BF16),
        ],
        compiler_params=params(16),
        name="project_msa",
    )(stack, weights.T)


def attend_kernel(width, at_ref, qkv_ref, mine_ref, other_ref, pen_ref, out_ref, bias_ref, value_ref):
    block = pl.program_id(0)
    columns, entries = qkv_ref.shape[0], qkv_ref.shape[1]
    lanes = qkv_ref.shape[3]
    take = out_ref.shape[0]
    length, _, _, tile, _ = mine_ref.shape
    first = at_ref[0] == 0

    @pl.when(block == 0)
    def _():
        ones = jnp.ones((lanes - width, lanes), F32)

        @pl.loop(0, entries)
        def _(s):
            for j in range(columns):
                part = jnp.concatenate([qkv_ref[j, s, 2 * width :].astype(F32), ones], axis=0)
                value_ref[s, j * lanes : (j + 1) * lanes] = part.T.astype(BF16)

    planes = take * lanes // (2 * tile)

    @pl.loop(0, planes)
    def _(q):
        plane = block * planes + q
        place = ring_place((plane + 2 * length - at_ref[2]) % length, length)
        side = jnp.bitwise_xor(plane // length, at_ref[1])
        upper = pl.ds(pl.multiple_of(q * 2 * tile, tile), tile)
        lower = pl.ds(pl.multiple_of(q * 2 * tile + tile, tile), tile)
        for j in range(columns):
            a = mine_ref[place, side, j].astype(F32)
            b = other_ref[place, side, j].astype(F32)
            at = slice(j * lanes, (j + 1) * lanes)
            pen = pen_ref[:, at]
            bias_ref[upper, at] = (jnp.where(first, a, b) + pen) * LOG2E
            bias_ref[lower, at] = (jnp.where(first, b, a) + pen) * LOG2E

    scale = width ** (-0.5) * LOG2E
    for s in range(entries):
        query = jnp.concatenate([qkv_ref[block * take + t, s, 0:width] for t in range(take)], axis=1)
        query = (query.astype(F32) * scale).T.astype(BF16)
        keys = jnp.concatenate([qkv_ref[j, s, width : 2 * width] for j in range(columns)], axis=1)
        logits = dot(query, keys, (1, 0)) + bias_ref[...]
        top = jnp.max(logits, axis=1, keepdims=True)
        weights = jnp.exp2(logits - top).astype(BF16)
        blended = dot(weights, value_ref[s], (1, 0))
        for t in range(take):
            part = blended[t * lanes : (t + 1) * lanes].T
            out_ref[t, s] = (part[:width] * (1.0 / part[width : width + 1])).astype(BF16)


def attend(at, qkv, mine, other, pen, width):
    columns, entries, _, lanes = qkv.shape
    take = 2
    return pl.pallas_call(
        functools.partial(attend_kernel, width),
        grid_spec=pltpu.PrefetchScalarGridSpec(
            num_scalar_prefetch=1,
            grid=(columns // take,),
            in_specs=[whole(qkv.shape), whole(mine.shape), whole(other.shape), whole(pen.shape)],
            out_specs=pl.BlockSpec((take, entries, width, lanes), lambda b, at: (b, 0, 0, 0)),
            scratch_shapes=[
                pltpu.VMEM((take * lanes, columns * lanes), F32),
                pltpu.VMEM((entries, columns * lanes, lanes), BF16),
            ],
        ),
        out_shape=jax.ShapeDtypeStruct((columns, entries, width, lanes), BF16),
        compiler_params=params(32),
        name="attend",
    )(at, qkv, mine, other, pen)


def sides_kernel(
    side, att_ref, gate_ref, stack_ref, mask_ref, wo_ref, wl_ref, wr_ref, out_ref, left_ref, right_ref, hold_ref
):
    step = pl.program_id(0)
    take, residues, features = stack_ref.shape
    gated = jnp.concatenate(
        [
            (
                att_ref[:, s].astype(F32).reshape(-1, residues) * sigmoid(gate_ref[s].astype(F32))
            ).astype(BF16)
            for s in range(take)
        ],
        axis=1,
    )
    stack = stack_ref[...].astype(F32).reshape(take * residues, features)
    updated = (stack + dot(gated, wo_ref[...], (0, 0))).astype(BF16)
    out_ref[...] = updated.reshape(take, residues, features)
    normed = standardize(updated, -1).astype(BF16)
    right = dot(wr_ref[...], normed, (1, 1))
    group = 128 // side
    spread = dot(normed, wl_ref[...], (1, 0))
    rows = lax.broadcasted_iota(jnp.int32, spread.shape, 0)
    lanes = lax.broadcasted_iota(jnp.int32, spread.shape, 1)
    spread = jnp.where(rows % group == lanes // side, spread, 0.0).astype(BF16)
    to = lax.broadcasted_iota(jnp.int32, (residues // group, residues), 0)
    of = lax.broadcasted_iota(jnp.int32, (residues // group, residues), 1)
    gather = jnp.where(of // group == to, 1.0, 0.0)
    tail = lax.broadcasted_iota(jnp.int32, (16, residues), 0)
    for s in range(take):
        mask = mask_ref[s]
        at = slice(s * residues, (s + 1) * residues)
        hold_ref[pl.ds(step * take + s, side, stride=8), :] = right[:, at] * mask
        hold_ref[pl.ds(side * 8 + step * take + s, 1), :] = mask
        left = dot((gather * mask).astype(BF16), spread[at], (1, 0))
        left_ref[s, 0 : residues // group] = left.astype(BF16)
        left_ref[s, residues // group :] = jnp.where(tail == 0, mask, 0.0).astype(BF16)

    @pl.when(step == pl.num_programs(0) - 1)
    def _():
        right_ref[...] = hold_ref[...].astype(BF16)


def sides(attended, gate, stack, mask, w_out, w_sides):
    entries, residues, features = stack.shape
    heads, _, width, _ = attended.shape
    side = w_sides.shape[1] // 2
    group = 128 // side
    rows = residues // group + 16
    take = 4
    return pl.pallas_call(
        functools.partial(sides_kernel, side),
        grid=(entries // take,),
        in_specs=[
            pl.BlockSpec((heads, take, width, residues), lambda s: (0, s, 0, 0)),
            pl.BlockSpec((take, features, residues), lambda s: (s, 0, 0)),
            pl.BlockSpec((take, residues, features), lambda s: (s, 0, 0)),
            pl.BlockSpec((take, 1, residues), lambda s: (s, 0, 0)),
            whole(w_out.shape),
            whole((features, 128)),
            whole((side, features)),
        ],
        out_specs=[
            pl.BlockSpec((take, residues, features), lambda s: (s, 0, 0)),
            pl.BlockSpec((take, rows, 128), lambda s: (s, 0, 0)),
            whole(((side + 1) * 8, residues)),
        ],
        out_shape=[
            jax.ShapeDtypeStruct(stack.shape, BF16),
            jax.ShapeDtypeStruct((entries, rows, 128), BF16),
            jax.ShapeDtypeStruct(((side + 1) * 8, residues), BF16),
        ],
        scratch_shapes=[pltpu.VMEM(((side + 1) * 8, residues), F32)],
        compiler_params=params(16),
        name="sides",
    )(
        attended,
        gate,
        stack,
        mask[:, None, :].astype(F32),
        w_out,
        jnp.tile(w_sides[:, :side], (1, group)),
        w_sides[:, side:].T,
    )


OUTER_CHUNKS = 4


def outer_kernel(
    side, at_ref, left_ref, lmask_ref, mine_ref, other_ref, couple_ref, live_ref, we_ref, wt_ref,
    mid_ref, l_ref, r_ref, right_ref, rmask_ref, rows_ref, x_ref, update_ref, count_ref,
):
    step = pl.program_id(0)
    rows, lanes = couple_ref.shape[0], couple_ref.shape[1]
    channels = couple_ref.shape[2]
    pair_rows = live_ref.shape[0]

    @pl.when(step == 0)
    def _():
        length, branches = mine_ref.shape[0], mine_ref.shape[1]

        @pl.loop(0, branches * length)
        def _(plane):
            place = ring_place((plane + branches * length - at_ref[2]) % length, length)
            which = jnp.bitwise_xor(plane // length, at_ref[1])
            at = pl.ds(pl.multiple_of(plane * 16, 16), 16)
            for d in range(side + 1):
                pair = [ref[place, which, d * 8 : (d + 1) * 8] for ref in (mine_ref, other_ref)]
                pair = jnp.concatenate(pair, axis=0)
                if d < side:
                    right_ref[d // 2, at, d % 2 * lanes : (d % 2 + 1) * lanes] = pair
                else:
                    rmask_ref[at, :] = pair

        count_ref[...] = 1.0 / (dot(lmask_ref[...], rmask_ref[...], (0, 0)) + 1.0)
        for t in range(left_ref.shape[0]):
            rows_ref[t * 128 : (t + 1) * 128] = left_ref[t].T

    @pl.when(step < OUTER_CHUNKS)
    def _():
        part = side // OUTER_CHUNKS
        for k in range(0, part, 2):
            sums = dot(rows_ref[...], right_ref[step * (part // 2) + k // 2], (1, 0)).astype(BF16)
            for i in range(pair_rows):
                for e in range(2):
                    x_ref[(k + e) * side : (k + e + 1) * side, i * lanes : (i + 1) * lanes] = sums[
                        i * side : (i + 1) * side, e * lanes : (e + 1) * lanes
                    ]
        added = dot(we_ref[step], x_ref[...], (1, 0))

        @pl.when(step == 0)
        def _():
            update_ref[...] = added

        @pl.when(step > 0)
        def _():
            update_ref[...] += added

    @pl.when(step >= OUTER_CHUNKS)
    def _():
        first = (step - OUTER_CHUNKS) * rows
        normed = []
        for i in range(rows):
            over = count_ref[pl.ds(at_ref[3] * pair_rows + first + i, 1), :]
            update = update_ref[:, pl.ds(pl.multiple_of((first + i) * lanes, lanes), lanes)]
            mid = couple_ref[i].astype(F32).T + update * over
            mid_ref[i] = mid
            normed.append(standardize(mid, 0).astype(BF16))
        normed = jnp.concatenate(normed, axis=1)
        for part, ref in ((0, l_ref), (2, r_ref)):
            gate = dot(wt_ref[part * channels : (part + 1) * channels], normed, (1, 0))
            value = dot(wt_ref[(part + 1) * channels : (part + 2) * channels], normed, (1, 0))
            both = sigmoid(gate) * value
            for i in range(rows):
                live = live_ref[pl.ds(first + i, 1), :]
                ref[i] = (both[:, i * lanes : (i + 1) * lanes] * live).astype(BF16)


def outer(at, left, lmask, mine, other, couple, live, w_exit, w_tri):
    _, entries, _ = left.shape
    pair_rows, lanes, channels = couple.shape
    rows = 8
    side = mine.shape[2] // 8 - 1
    move = lambda t, at: (jnp.maximum(t - OUTER_CHUNKS, 0), 0, 0)
    tile = pl.BlockSpec((rows, channels, lanes), move)
    depth = side * side // OUTER_CHUNKS
    w_exit = w_exit.reshape(side, side, channels).transpose(1, 0, 2)
    w_exit = w_exit.reshape(OUTER_CHUNKS, depth, channels).transpose(0, 2, 1)
    return pl.pallas_call(
        functools.partial(outer_kernel, side),
        grid_spec=pltpu.PrefetchScalarGridSpec(
            num_scalar_prefetch=1,
            grid=(OUTER_CHUNKS + pair_rows // rows,),
            in_specs=[
                whole(left.shape),
                whole(lmask.shape),
                whole(mine.shape),
                whole(other.shape),
                pl.BlockSpec((rows, lanes, channels), move),
                whole(live.shape),
                whole(w_exit.shape),
                whole((4 * channels, channels)),
            ],
            out_specs=[tile, tile, tile],
            scratch_shapes=[
                pltpu.VMEM((side // 2, entries, 2 * lanes), BF16),
                pltpu.VMEM((entries, lanes), BF16),
                pltpu.VMEM((pair_rows * side, entries), BF16),
                pltpu.VMEM((depth, pair_rows * lanes), BF16),
                pltpu.VMEM((channels, pair_rows * lanes), F32),
                pltpu.VMEM((128, lanes), F32),
            ],
        ),
        out_shape=[
            jax.ShapeDtypeStruct((pair_rows, channels, lanes), F32),
            jax.ShapeDtypeStruct((pair_rows, channels, lanes), BF16),
            jax.ShapeDtypeStruct((pair_rows, channels, lanes), BF16),
        ],
        compiler_params=params(40),
        name="outer",
    )(at, left, lmask, mine, other, couple, live, w_exit, w_tri.T)


def triangle_kernel(me_ref, l_ref, mine_ref, other_ref, out_ref):
    planes, columns, tile, lanes = l_ref.shape
    first = me_ref[0] == 0
    joined = lambda ref, p: jnp.concatenate([ref[p, k] for k in range(columns)], axis=1)
    rights = []
    for p in range(mine_ref.shape[0]):
        a, b = joined(mine_ref, p), joined(other_ref, p)
        rights += [jnp.where(first, a, b), jnp.where(first, b, a)]
    right = jnp.concatenate(rights, axis=0)
    per = lanes // (2 * tile)
    for p in range(0, planes, 4):
        left = jnp.concatenate([joined(l_ref, p + q) for q in range(4)], axis=0)
        product = dot(left, right, (1, 1)).astype(BF16)
        for q in range(4):
            for n in range(mine_ref.shape[0] // per):
                out_ref[p + q, n] = product[
                    q * tile : (q + 1) * tile, n * lanes : (n + 1) * lanes
                ]


def triangle(me, left, mine, other):
    planes, columns, tile, lanes = left.shape
    per = lanes // (2 * tile)
    take = 2
    spec = pl.BlockSpec((per * take, columns, tile, lanes), lambda n, me: (n, 0, 0, 0))
    return pl.pallas_call(
        triangle_kernel,
        grid_spec=pltpu.PrefetchScalarGridSpec(
            num_scalar_prefetch=1,
            grid=(columns // take,),
            in_specs=[whole(left.shape), spec, spec],
            out_specs=pl.BlockSpec((planes, take, tile, lanes), lambda n, me: (0, n, 0, 0)),
        ),
        out_shape=jax.ShapeDtypeStruct(left.shape, BF16),
        compiler_params=params(20),
        name="triangle",
    )(me, left, mine, other)


def switch_kernel(mid_ref, ws_ref, gate_ref):
    rows, _, lanes = mid_ref.shape
    normed = [standardize(mid_ref[i], 0).astype(BF16) for i in range(rows)]
    gate = sigmoid(dot(ws_ref[...], jnp.concatenate(normed, axis=1), (1, 0)))
    for i in range(rows):
        gate_ref[i] = gate[:, i * lanes : (i + 1) * lanes]


def switch(mid, w_switch):
    pair_rows, channels, lanes = mid.shape
    tile = pl.BlockSpec((2, channels, lanes), lambda t: (t, 0, 0))
    return pl.pallas_call(
        switch_kernel,
        grid=(pair_rows // 2,),
        in_specs=[tile, whole(w_switch.shape)],
        out_specs=tile,
        out_shape=jax.ShapeDtypeStruct(mid.shape, F32),
        compiler_params=params(16),
        name="switch",
    )(mid, w_switch.T)


def finish_kernel(prod_ref, mid_ref, gate_ref, wo_ref, out_ref, mixed_ref):
    step = pl.program_id(0)
    channels, pair_rows, lanes = prod_ref.shape
    rows = mid_ref.shape[0]

    @pl.when(step == 0)
    def _():
        zero = jnp.zeros((pair_rows, lanes), F32)
        take = 16

        def add(k, total):
            for c in range(take):
                total = total + prod_ref[k * take + c].astype(F32)
            return total

        mean = lax.fori_loop(0, channels // take, add, zero) / channels

        def add_square(k, total):
            for c in range(take):
                centered = prod_ref[k * take + c].astype(F32) - mean
                total = total + centered * centered
            return total

        spread = lax.fori_loop(0, channels // take, add_square, zero) / channels
        inverse = lax.rsqrt(spread + EPSILON)

        @pl.loop(0, channels // take)
        def _(k):
            for c in range(take):
                row = pl.multiple_of((k * take + c) * pair_rows, pair_rows)
                mixed_ref[pl.ds(row, pair_rows), :] = (
                    prod_ref[k * take + c].astype(F32) - mean
                ) * inverse

    mixed = [
        mixed_ref[pl.ds(step * rows + i, channels, stride=pair_rows), :].astype(BF16)
        for i in range(rows)
    ]
    update = dot(wo_ref[...], jnp.concatenate(mixed, axis=1), (1, 0))
    for i in range(rows):
        result = mid_ref[i] + update[:, i * lanes : (i + 1) * lanes] * gate_ref[i]
        out_ref[i] = result.T.astype(BF16)


def finish(product, mid, gate, w_out):
    channels, pair_rows, lanes = product.shape
    rows = 8
    tile = pl.BlockSpec((rows, channels, lanes), lambda t: (t, 0, 0))
    return pl.pallas_call(
        finish_kernel,
        grid=(pair_rows // rows,),
        in_specs=[whole(product.shape), tile, tile, whole(w_out.shape)],
        out_specs=pl.BlockSpec((rows, lanes, channels), lambda t: (t, 0, 0)),
        out_shape=jax.ShapeDtypeStruct((pair_rows, lanes, channels), BF16),
        scratch_shapes=[pltpu.VMEM((channels * pair_rows, lanes), F32)],
        compiler_params=params(24),
        name="finish",
    )(product, mid, gate, w_out.T)


def swap(x):
    return lax.ppermute(x, "row_1", SWAP)


def exchange(x, axes):
    return lax.all_to_all(x, axes, 0, 0, tiled=True)


def ring_gather(x):
    n = lax.axis_size("row_0")

    def shift(y, by):
        return lax.ppermute(y, "row_0", tuple((k, (k + by) % n) for k in range(n)))

    pair = jnp.stack([x, lax.ppermute(x, "branch", SWAP)])
    above, below, above_2, below_2 = (shift(pair, by) for by in (1, -1, 2, -2))
    above_3, below_3 = shift(above_2, 1), shift(below_2, -1)
    last = [shift(above_2[:1], 2), shift(below_2[1:], -2)]
    return jnp.stack([pair, above, below, above_2, below_2, above_3, below_3, jnp.concatenate(last)])


def ring_place(ahead, n):
    return jnp.where(ahead <= n // 2, jnp.maximum(2 * ahead - (ahead == n // 2), 0), 2 * (n - ahead) - 1)


def repeated(x, n):
    return jnp.broadcast_to(x[None], (n, *x.shape))


def shards(
    homolog_stack,
    couple_tensor,
    amino_occupancy,
    homolog_occupancy,
    focus_entry_coefficients,
    couple_offset_coefficients,
    focus_exit_coefficients,
    tensor_entry_coefficients,
    tensor_exit_coefficients,
    trio_entry_coefficients,
    trio_exit_switch,
    trio_exit_coefficients,
):
    _, residues, features = homolog_stack.shape
    pair_rows, pair_cols, pair_width = couple_tensor.shape
    heads = couple_offset_coefficients.shape[1]
    width = features // heads
    side = tensor_entry_coefficients.shape[1] // 2
    planes = lax.axis_size("branch") * lax.axis_size("row_0")
    chan = lax.axis_size("chan")
    core = lax.axis_index("row_1").astype(jnp.int32)
    row = lax.axis_index(BRANCH_ROW).astype(jnp.int32)
    place = [core, lax.axis_index("branch"), lax.axis_index("row_0"), row % 4]
    at = jnp.stack([p.astype(jnp.int32) for p in place])
    me = core.reshape(1)
    live = amino_occupancy.astype(F32)
    live_rows = lax.dynamic_slice_in_dim(live, row * pair_rows, pair_rows)
    live_cols = lax.dynamic_slice_in_dim(live, lax.axis_index("chan") * pair_cols, pair_cols)
    penalty = ((live - 1.0) * MASKED)[None, :]

    pair_norm = standardize(couple_tensor, -1).astype(BF16)
    bias = jnp.einsum(
        "ijc,ch->hij", pair_norm, couple_offset_coefficients, preferred_element_type=F32
    ).astype(BF16)
    bias = exchange(bias, "chan")
    bias = ring_gather(bias)
    bias_other = swap(bias)

    qkv, gate = project_msa(homolog_stack, focus_entry_coefficients, heads)
    qkv = exchange(qkv, "chan")
    attended = attend(at, qkv, bias, bias_other, penalty, width)
    attended = exchange(attended, "chan")

    homolog_after_update, left, right = sides(
        attended,
        gate,
        homolog_stack,
        homolog_occupancy,
        focus_exit_coefficients,
        tensor_entry_coefficients,
    )
    right = ring_gather(right)
    right_other = swap(right)
    members = 2 * planes
    packed_rows = residues * side // 128
    steps = chan * packed_rows // members
    left = exchange(left, "chan")
    left = jnp.concatenate(
        [
            left[:, :packed_rows].reshape(members, steps, 128),
            jnp.repeat(left[:, packed_rows : packed_rows + 8], members // chan, axis=0),
        ],
        axis=1,
    )
    left = exchange(left, BRANCH_ROW)
    left = left[:, : steps + 1].reshape(planes, 2, steps + 1, 128)
    left = jnp.where(core == 0, left, left[:, ::-1]).reshape(members, steps + 1, 128)
    left = repeated(left.transpose(1, 0, 2), chan)
    left = exchange(left, "chan")
    left = left.transpose(1, 2, 0, 3).reshape(steps + 1, members * chan, 128)
    mid, left_tri, right_tri = outer(
        at,
        left[:steps],
        left[steps],
        right,
        right_other,
        couple_tensor,
        live_rows[:, None] * live_cols[None, :],
        tensor_exit_coefficients,
        trio_entry_coefficients,
    )
    operands = jnp.stack([left_tri, right_tri]).transpose(2, 0, 1, 3)
    operands = exchange(operands, CHIPS)
    grid = (planes, chan, pair_rows, pair_cols)
    left_tri, right_tri = operands[:, 0].reshape(grid), operands[:, 1].reshape(grid)
    product = triangle(me, left_tri, right_tri, swap(right_tri))
    product = exchange(product.reshape(pair_width, pair_rows, pair_cols), CHIPS)
    gate = switch(mid, trio_exit_switch)
    pair_result = finish(product, mid, gate, trio_exit_coefficients)
    return (homolog_after_update, pair_result)


def solution(mesh):
    torus = Mesh(
        mesh.devices.reshape(mesh.shape["branch"], 8, 2, mesh.shape["chan"]),
        ("branch", "row_0", "row_1", "chan"),
    )

    return jax.shard_map(
        shards,
        mesh=torus,
        in_specs=(
            P(BRANCH_ROW, "chan", None),
            P(BRANCH_ROW, "chan", None),
            P(),
            P(BRANCH_ROW, "chan"),
            *(P() for _ in range(8)),
        ),
        out_specs=(P(BRANCH_ROW, "chan", None), P(BRANCH_ROW, "chan", None)),
        check_vma=False,
    )
```

```python
import functools

import jax
import jax.numpy as jnp
from jax import lax
from jax.experimental import pallas as pl
from jax.experimental.pallas import tpu as pltpu
from jax.sharding import Mesh
from jax.sharding import PartitionSpec as P


BRANCH_ROW = ("branch", "row_0", "row_1")
CHIPS = ("branch", "row_0", "chan")
SWAP = ((0, 1), (1, 0))
EPSILON = 1e-05
MASKED = 1000000000.0
LOG2E = 1.4426950408889634
BF16 = jnp.bfloat16
F32 = jnp.float32


def params(mebibytes):
    return pltpu.CompilerParams(
        dimension_semantics=("arbitrary",), vmem_limit_bytes=mebibytes * 1024 * 1024
    )


def dot(a, b, dims):
    return lax.dot_general(a, b, ((dims[:1], dims[1:]), ((), ())), preferred_element_type=F32)


def standardize(values, axis):
    values = values.astype(F32)
    centered = values - jnp.mean(values, axis=axis, keepdims=True)
    spread = jnp.mean(centered * centered, axis=axis, keepdims=True)
    return centered * lax.rsqrt(spread + EPSILON)


def sigmoid(x):
    return 1.0 / (1.0 + jnp.exp(-x))


def whole(shape):
    return pl.BlockSpec(shape, lambda *_: (0,) * len(shape))


def bias_kernel(x_ref, w_ref, out_ref, hold_ref):
    step = pl.program_id(0)
    rows, lanes, channels = x_ref.shape
    heads, pair_rows, _ = out_ref.shape
    normed = standardize(x_ref[...].reshape(rows * lanes, channels), -1).astype(BF16)
    bias = dot(w_ref[...], normed, (1, 1))
    for i in range(rows):
        hold_ref[pl.ds(step * rows + i, heads, stride=pair_rows), :] = bias[
            :, i * lanes : (i + 1) * lanes
        ]

    @pl.when(step == pl.num_programs(0) - 1)
    def _():
        out_ref[...] = hold_ref[...].astype(BF16).reshape(heads, pair_rows, lanes)


def pair_bias(couple, weights):
    pair_rows, lanes, channels = couple.shape
    heads = weights.shape[1]
    rows = 8
    return pl.pallas_call(
        bias_kernel,
        grid=(pair_rows // rows,),
        in_specs=[
            pl.BlockSpec((rows, lanes, channels), lambda t: (t, 0, 0)),
            whole((heads, channels)),
        ],
        out_specs=whole((heads, pair_rows, lanes)),
        out_shape=jax.ShapeDtypeStruct((heads, pair_rows, lanes), BF16),
        scratch_shapes=[pltpu.VMEM((heads * pair_rows, lanes), F32)],
        compiler_params=params(16),
        name="pair_bias",
    )(couple, weights.T)


def project_kernel(heads, width, x_ref, w_ref, qkv_ref, gate_ref):
    entries, residues, features = x_ref.shape
    normed = standardize(x_ref[...].reshape(entries * residues, features), -1).astype(BF16)
    packed = dot(w_ref[...], normed, (1, 1)).astype(BF16)
    for s in range(entries):
        at = slice(s * residues, (s + 1) * residues)
        for h in range(heads):
            base = h * 4 * width
            qkv_ref[h, s] = packed[base : base + 3 * width, at]
            gate_ref[s, h * width : (h + 1) * width] = packed[
                base + 3 * width : base + 4 * width, at
            ]


def project_msa(stack, weights, heads):
    entries, residues, features = stack.shape
    width = features // heads
    take = 2
    return pl.pallas_call(
        functools.partial(project_kernel, heads, width),
        grid=(entries // take,),
        in_specs=[
            pl.BlockSpec((take, residues, features), lambda s: (s, 0, 0)),
            whole((4 * features, features)),
        ],
        out_specs=[
            pl.BlockSpec((heads, take, 3 * width, residues), lambda s: (0, s, 0, 0)),
            pl.BlockSpec((take, features, residues), lambda s: (s, 0, 0)),
        ],
        out_shape=[
            jax.ShapeDtypeStruct((heads, entries, 3 * width, residues), BF16),
            jax.ShapeDtypeStruct((entries, features, residues), BF16),
        ],
        compiler_params=params(16),
        name="project_msa",
    )(stack, weights.T)


def attend_kernel(width, at_ref, qkv_ref, mine_ref, other_ref, pen_ref, out_ref, bias_ref, value_ref):
    block = pl.program_id(0)
    columns, entries = qkv_ref.shape[0], qkv_ref.shape[1]
    lanes = qkv_ref.shape[3]
    take = out_ref.shape[0]
    length, _, _, tile, _ = mine_ref.shape
    first = at_ref[0] == 0

    @pl.when(block == 0)
    def _():
        ones = jnp.ones((lanes - width, lanes), F32)

        @pl.loop(0, entries)
        def _(s):
            for j in range(columns):
                part = jnp.concatenate([qkv_ref[j, s, 2 * width :].astype(F32), ones], axis=0)
                value_ref[s, j * lanes : (j + 1) * lanes] = part.T.astype(BF16)

    planes = take * lanes // (2 * tile)

    @pl.loop(0, planes)
    def _(q):
        plane = block * planes + q
        place = ring_place((plane + 2 * length - at_ref[2]) % length, length)
        side = jnp.bitwise_xor(plane // length, at_ref[1])
        upper = pl.ds(pl.multiple_of(q * 2 * tile, tile), tile)
        lower = pl.ds(pl.multiple_of(q * 2 * tile + tile, tile), tile)
        for j in range(columns):
            a = mine_ref[place, side, j].astype(F32)
            b = other_ref[place, side, j].astype(F32)
            at = slice(j * lanes, (j + 1) * lanes)
            pen = pen_ref[:, at]
            bias_ref[upper, at] = (jnp.where(first, a, b) + pen) * LOG2E
            bias_ref[lower, at] = (jnp.where(first, b, a) + pen) * LOG2E

    scale = width ** (-0.5) * LOG2E
    for s in range(entries):
        query = jnp.concatenate([qkv_ref[block * take + t, s, 0:width] for t in range(take)], axis=1)
        query = (query.astype(F32) * scale).T.astype(BF16)
        keys = jnp.concatenate([qkv_ref[j, s, width : 2 * width] for j in range(columns)], axis=1)
        logits = dot(query, keys, (1, 0)) + bias_ref[...]
        top = jnp.max(logits, axis=1, keepdims=True)
        weights = jnp.exp2(logits - top).astype(BF16)
        blended = dot(weights, value_ref[s], (1, 0))
        for t in range(take):
            part = blended[t * lanes : (t + 1) * lanes].T
            out_ref[t, s] = (part[:width] * (1.0 / part[width : width + 1])).astype(BF16)


def attend(at, qkv, mine, other, pen, width):
    columns, entries, _, lanes = qkv.shape
    take = 4
    return pl.pallas_call(
        functools.partial(attend_kernel, width),
        grid_spec=pltpu.PrefetchScalarGridSpec(
            num_scalar_prefetch=1,
            grid=(columns // take,),
            in_specs=[whole(qkv.shape), whole(mine.shape), whole(other.shape), whole(pen.shape)],
            out_specs=pl.BlockSpec((take, entries, width, lanes), lambda b, at: (b, 0, 0, 0)),
            scratch_shapes=[
                pltpu.VMEM((take * lanes, columns * lanes), F32),
                pltpu.VMEM((entries, columns * lanes, lanes), BF16),
            ],
        ),
        out_shape=jax.ShapeDtypeStruct((columns, entries, width, lanes), BF16),
        compiler_params=params(48),
        name="attend",
    )(at, qkv, mine, other, pen)


def sides_kernel(
    side, att_ref, gate_ref, stack_ref, mask_ref, wo_ref, wl_ref, wr_ref, out_ref, left_ref, right_ref, hold_ref
):
    step = pl.program_id(0)
    take, residues, features = stack_ref.shape
    gated = jnp.concatenate(
        [
            (
                att_ref[:, s].astype(F32).reshape(-1, residues) * sigmoid(gate_ref[s].astype(F32))
            ).astype(BF16)
            for s in range(take)
        ],
        axis=1,
    )
    stack = stack_ref[...].astype(F32).reshape(take * residues, features)
    updated = (stack + dot(gated, wo_ref[...], (0, 0))).astype(BF16)
    out_ref[...] = updated.reshape(take, residues, features)
    normed = standardize(updated, -1).astype(BF16)
    right = dot(wr_ref[...], normed, (1, 1))
    group = 128 // side
    spread = dot(normed, wl_ref[...], (1, 0))
    rows = lax.broadcasted_iota(jnp.int32, spread.shape, 0)
    lanes = lax.broadcasted_iota(jnp.int32, spread.shape, 1)
    spread = jnp.where(rows % group == lanes // side, spread, 0.0).astype(BF16)
    to = lax.broadcasted_iota(jnp.int32, (residues // group, residues), 0)
    of = lax.broadcasted_iota(jnp.int32, (residues // group, residues), 1)
    gather = jnp.where(of // group == to, 1.0, 0.0)
    tail = lax.broadcasted_iota(jnp.int32, (16, residues), 0)
    for s in range(take):
        mask = mask_ref[s]
        at = slice(s * residues, (s + 1) * residues)
        hold_ref[pl.ds(step * take + s, side, stride=8), :] = right[:, at] * mask
        hold_ref[pl.ds(side * 8 + step * take + s, 1), :] = mask
        left = dot((gather * mask).astype(BF16), spread[at], (1, 0))
        left_ref[s, 0 : residues // group] = left.astype(BF16)
        left_ref[s, residues // group :] = jnp.where(tail == 0, mask, 0.0).astype(BF16)

    @pl.when(step == pl.num_programs(0) - 1)
    def _():
        right_ref[...] = hold_ref[...].astype(BF16)


def sides(attended, gate, stack, mask, w_out, w_sides):
    entries, residues, features = stack.shape
    heads, _, width, _ = attended.shape
    side = w_sides.shape[1] // 2
    group = 128 // side
    rows = residues // group + 16
    take = 4
    return pl.pallas_call(
        functools.partial(sides_kernel, side),
        grid=(entries // take,),
        in_specs=[
            pl.BlockSpec((heads, take, width, residues), lambda s: (0, s, 0, 0)),
            pl.BlockSpec((take, features, residues), lambda s: (s, 0, 0)),
            pl.BlockSpec((take, residues, features), lambda s: (s, 0, 0)),
            pl.BlockSpec((take, 1, residues), lambda s: (s, 0, 0)),
            whole(w_out.shape),
            whole((features, 128)),
            whole((side, features)),
        ],
        out_specs=[
            pl.BlockSpec((take, residues, features), lambda s: (s, 0, 0)),
            pl.BlockSpec((take, rows, 128), lambda s: (s, 0, 0)),
            whole(((side + 1) * 8, residues)),
        ],
        out_shape=[
            jax.ShapeDtypeStruct(stack.shape, BF16),
            jax.ShapeDtypeStruct((entries, rows, 128), BF16),
            jax.ShapeDtypeStruct(((side + 1) * 8, residues), BF16),
        ],
        scratch_shapes=[pltpu.VMEM(((side + 1) * 8, residues), F32)],
        compiler_params=params(16),
        name="sides",
    )(
        attended,
        gate,
        stack,
        mask[:, None, :].astype(F32),
        w_out,
        jnp.tile(w_sides[:, :side], (1, group)),
        w_sides[:, side:].T,
    )


OUTER_CHUNKS = 4


def outer_kernel(
    side, at_ref, left_ref, mine_ref, other_ref, couple_ref, live_ref, we_ref, wt_ref,
    mid_ref, l_ref, r_ref, right_ref, rmask_ref, rows_ref, x_ref, update_ref, count_ref,
):
    step = pl.program_id(0)
    rows, lanes = couple_ref.shape[0], couple_ref.shape[1]
    channels = couple_ref.shape[2]
    pair_rows = live_ref.shape[0]
    entries = rmask_ref.shape[0]

    @pl.when(step == 0)
    def _():
        length, branches = mine_ref.shape[0], mine_ref.shape[1]

        @pl.loop(0, branches * length)
        def _(plane):
            place = ring_place((plane + branches * length - at_ref[2]) % length, length)
            which = jnp.bitwise_xor(plane // length, at_ref[1])
            at = pl.ds(pl.multiple_of(plane * 16, 16), 16)
            for d in range(side + 1):
                pair = [ref[place, which, d * 8 : (d + 1) * 8] for ref in (mine_ref, other_ref)]
                pair = jnp.concatenate(pair, axis=0)
                if d < side:
                    right_ref[d // 2, at, d % 2 * lanes : (d % 2 + 1) * lanes] = pair
                else:
                    rmask_ref[at, :] = pair

        columns, tiles, members, _ = left_ref.shape
        given = lax.broadcasted_iota(jnp.int32, (entries, entries), 0)
        wanted = lax.broadcasted_iota(jnp.int32, (entries, entries), 1)
        member = jnp.bitwise_xor(given % members, at_ref[0])
        order = jnp.where(member * columns + given // members == wanted, 1.0, 0.0).astype(BF16)
        for t in range(tiles):
            rows_in = jnp.concatenate([left_ref[c, t] for c in range(columns)], axis=0)
            turned = dot(rows_in, order, (0, 0)).astype(BF16)
            if t < tiles - 1:
                rows_ref[t * 128 : (t + 1) * 128] = turned
            else:
                count_ref[...] = 1.0 / (dot(turned, rmask_ref[...], (1, 0)) + 1.0)

    @pl.when(step < OUTER_CHUNKS)
    def _():
        part = side // OUTER_CHUNKS
        for k in range(0, part, 2):
            sums = dot(rows_ref[...], right_ref[step * (part // 2) + k // 2], (1, 0)).astype(BF16)
            for i in range(pair_rows):
                for e in range(2):
                    x_ref[(k + e) * side : (k + e + 1) * side, i * lanes : (i + 1) * lanes] = sums[
                        i * side : (i + 1) * side, e * lanes : (e + 1) * lanes
                    ]
        added = dot(we_ref[step], x_ref[...], (1, 0))

        @pl.when(step == 0)
        def _():
            update_ref[...] = added

        @pl.when(step > 0)
        def _():
            update_ref[...] += added

    @pl.when(step >= OUTER_CHUNKS)
    def _():
        first = (step - OUTER_CHUNKS) * rows
        normed = []
        for i in range(rows):
            over = count_ref[pl.ds(at_ref[3] * pair_rows + first + i, 1), :]
            update = update_ref[:, pl.ds(pl.multiple_of((first + i) * lanes, lanes), lanes)]
            mid = couple_ref[i].astype(F32).T + update * over
            mid_ref[i] = mid
            normed.append(standardize(mid, 0).astype(BF16))
        normed = jnp.concatenate(normed, axis=1)
        for part, ref in ((0, l_ref), (2, r_ref)):
            gate = dot(wt_ref[part * channels : (part + 1) * channels], normed, (1, 0))
            value = dot(wt_ref[(part + 1) * channels : (part + 2) * channels], normed, (1, 0))
            both = sigmoid(gate) * value
            for i in range(rows):
                live = live_ref[pl.ds(first + i, 1), :]
                ref[i] = (both[:, i * lanes : (i + 1) * lanes] * live).astype(BF16)


def outer(at, left, mine, other, couple, live, w_exit, w_tri):
    entries = left.shape[0] * left.shape[2]
    pair_rows, lanes, channels = couple.shape
    rows = 8
    side = mine.shape[2] // 8 - 1
    move = lambda t, at: (jnp.maximum(t - OUTER_CHUNKS, 0), 0, 0)
    tile = pl.BlockSpec((rows, channels, lanes), move)
    depth = side * side // OUTER_CHUNKS
    w_exit = w_exit.reshape(side, side, channels).transpose(1, 0, 2)
    w_exit = w_exit.reshape(OUTER_CHUNKS, depth, channels).transpose(0, 2, 1)
    return pl.pallas_call(
        functools.partial(outer_kernel, side),
        grid_spec=pltpu.PrefetchScalarGridSpec(
            num_scalar_prefetch=1,
            grid=(OUTER_CHUNKS + pair_rows // rows,),
            in_specs=[
                whole(left.shape),
                whole(mine.shape),
                whole(other.shape),
                pl.BlockSpec((rows, lanes, channels), move),
                whole(live.shape),
                whole(w_exit.shape),
                whole((4 * channels, channels)),
            ],
            out_specs=[tile, tile, tile],
            scratch_shapes=[
                pltpu.VMEM((side // 2, entries, 2 * lanes), BF16),
                pltpu.VMEM((entries, lanes), BF16),
                pltpu.VMEM((pair_rows * side, entries), BF16),
                pltpu.VMEM((depth, pair_rows * lanes), BF16),
                pltpu.VMEM((channels, pair_rows * lanes), F32),
                pltpu.VMEM((128, lanes), F32),
            ],
        ),
        out_shape=[
            jax.ShapeDtypeStruct((pair_rows, channels, lanes), F32),
            jax.ShapeDtypeStruct((pair_rows, channels, lanes), BF16),
            jax.ShapeDtypeStruct((pair_rows, channels, lanes), BF16),
        ],
        compiler_params=params(40),
        name="outer",
    )(at, left, mine, other, couple, live, w_exit, w_tri.T)


def triangle_kernel(me_ref, l_ref, mine_ref, other_ref, out_ref):
    planes, columns, tile, lanes = l_ref.shape
    first = me_ref[0] == 0
    joined = lambda ref, p: jnp.concatenate([ref[p, k] for k in range(columns)], axis=1)
    rights = []
    for p in range(mine_ref.shape[0]):
        a, b = joined(mine_ref, p), joined(other_ref, p)
        rights += [jnp.where(first, a, b), jnp.where(first, b, a)]
    right = jnp.concatenate(rights, axis=0)
    per = lanes // (2 * tile)
    for p in range(0, planes, 4):
        left = jnp.concatenate([joined(l_ref, p + q) for q in range(4)], axis=0)
        product = dot(left, right, (1, 1)).astype(BF16)
        for q in range(4):
            for n in range(mine_ref.shape[0] // per):
                out_ref[p + q, n] = product[
                    q * tile : (q + 1) * tile, n * lanes : (n + 1) * lanes
                ]


def triangle(me, left, mine, other):
    planes, columns, tile, lanes = left.shape
    per = lanes // (2 * tile)
    take = 2
    spec = pl.BlockSpec((per * take, columns, tile, lanes), lambda n, me: (n, 0, 0, 0))
    return pl.pallas_call(
        triangle_kernel,
        grid_spec=pltpu.PrefetchScalarGridSpec(
            num_scalar_prefetch=1,
            grid=(columns // take,),
            in_specs=[whole(left.shape), spec, spec],
            out_specs=pl.BlockSpec((planes, take, tile, lanes), lambda n, me: (0, n, 0, 0)),
        ),
        out_shape=jax.ShapeDtypeStruct(left.shape, BF16),
        compiler_params=params(20),
        name="triangle",
    )(me, left, mine, other)


def switch_kernel(mid_ref, ws_ref, gate_ref):
    rows, _, lanes = mid_ref.shape
    normed = [standardize(mid_ref[i], 0).astype(BF16) for i in range(rows)]
    gate = sigmoid(dot(ws_ref[...], jnp.concatenate(normed, axis=1), (1, 0)))
    for i in range(rows):
        gate_ref[i] = gate[:, i * lanes : (i + 1) * lanes]


def switch(mid, w_switch):
    pair_rows, channels, lanes = mid.shape
    tile = pl.BlockSpec((2, channels, lanes), lambda t: (t, 0, 0))
    return pl.pallas_call(
        switch_kernel,
        grid=(pair_rows // 2,),
        in_specs=[tile, whole(w_switch.shape)],
        out_specs=tile,
        out_shape=jax.ShapeDtypeStruct(mid.shape, F32),
        compiler_params=params(16),
        name="switch",
    )(mid, w_switch.T)


def finish_kernel(prod_ref, mid_ref, gate_ref, wo_ref, out_ref, mixed_ref):
    step = pl.program_id(0)
    channels, pair_rows, lanes = prod_ref.shape
    rows = mid_ref.shape[0]

    @pl.when(step == 0)
    def _():
        zero = jnp.zeros((pair_rows, lanes), F32)
        take = 16

        def add(k, total):
            for c in range(take):
                total = total + prod_ref[k * take + c].astype(F32)
            return total

        mean = lax.fori_loop(0, channels // take, add, zero) / channels

        def add_square(k, total):
            for c in range(take):
                centered = prod_ref[k * take + c].astype(F32) - mean
                total = total + centered * centered
            return total

        spread = lax.fori_loop(0, channels // take, add_square, zero) / channels
        inverse = lax.rsqrt(spread + EPSILON)

        @pl.loop(0, channels // take)
        def _(k):
            for c in range(take):
                row = pl.multiple_of((k * take + c) * pair_rows, pair_rows)
                mixed_ref[pl.ds(row, pair_rows), :] = (
                    prod_ref[k * take + c].astype(F32) - mean
                ) * inverse

    mixed = [
        mixed_ref[pl.ds(step * rows + i, channels, stride=pair_rows), :].astype(BF16)
        for i in range(rows)
    ]
    update = dot(wo_ref[...], jnp.concatenate(mixed, axis=1), (1, 0))
    for i in range(rows):
        result = mid_ref[i] + update[:, i * lanes : (i + 1) * lanes] * gate_ref[i]
        out_ref[i] = result.T.astype(BF16)


def finish(product, mid, gate, w_out):
    channels, pair_rows, lanes = product.shape
    rows = 8
    tile = pl.BlockSpec((rows, channels, lanes), lambda t: (t, 0, 0))
    return pl.pallas_call(
        finish_kernel,
        grid=(pair_rows // rows,),
        in_specs=[whole(product.shape), tile, tile, whole(w_out.shape)],
        out_specs=pl.BlockSpec((rows, lanes, channels), lambda t: (t, 0, 0)),
        out_shape=jax.ShapeDtypeStruct((pair_rows, lanes, channels), BF16),
        scratch_shapes=[pltpu.VMEM((channels * pair_rows, lanes), F32)],
        compiler_params=params(24),
        name="finish",
    )(product, mid, gate, w_out.T)


def swap(x):
    return lax.ppermute(x, "row_1", SWAP)


def exchange(x, axes):
    return lax.all_to_all(x, axes, 0, 0, tiled=True)


def ring_gather(x):
    n = lax.axis_size("row_0")

    def shift(y, by):
        return lax.ppermute(y, "row_0", tuple((k, (k + by) % n) for k in range(n)))

    pair = jnp.stack([x, lax.ppermute(x, "branch", SWAP)])
    above, below, above_2, below_2 = (shift(pair, by) for by in (1, -1, 2, -2))
    above_3, below_3 = shift(above_2, 1), shift(below_2, -1)
    last = [shift(above_2[:1], 2), shift(below_2[1:], -2)]
    return jnp.stack([pair, above, below, above_2, below_2, above_3, below_3, jnp.concatenate(last)])


def ring_place(ahead, n):
    return jnp.where(ahead <= n // 2, jnp.maximum(2 * ahead - (ahead == n // 2), 0), 2 * (n - ahead) - 1)


def repeated(x, n):
    return jnp.broadcast_to(x[None], (n, *x.shape))


def shards(
    homolog_stack,
    couple_tensor,
    amino_occupancy,
    homolog_occupancy,
    focus_entry_coefficients,
    couple_offset_coefficients,
    focus_exit_coefficients,
    tensor_entry_coefficients,
    tensor_exit_coefficients,
    trio_entry_coefficients,
    trio_exit_switch,
    trio_exit_coefficients,
):
    _, residues, features = homolog_stack.shape
    pair_rows, pair_cols, pair_width = couple_tensor.shape
    heads = couple_offset_coefficients.shape[1]
    width = features // heads
    side = tensor_entry_coefficients.shape[1] // 2
    planes = lax.axis_size("branch") * lax.axis_size("row_0")
    chan = lax.axis_size("chan")
    core = lax.axis_index("row_1").astype(jnp.int32)
    row = lax.axis_index(BRANCH_ROW).astype(jnp.int32)
    place = [core, lax.axis_index("branch"), lax.axis_index("row_0"), row % 4]
    at = jnp.stack([p.astype(jnp.int32) for p in place])
    me = core.reshape(1)
    live = amino_occupancy.astype(F32)
    live_rows = lax.dynamic_slice_in_dim(live, row * pair_rows, pair_rows)
    live_cols = lax.dynamic_slice_in_dim(live, lax.axis_index("chan") * pair_cols, pair_cols)
    penalty = ((live - 1.0) * MASKED)[None, :]

    bias = pair_bias(couple_tensor, couple_offset_coefficients)
    bias = exchange(bias, "chan")
    bias = ring_gather(bias)
    bias_other = swap(bias)

    qkv, gate = project_msa(homolog_stack, focus_entry_coefficients, heads)
    qkv = exchange(qkv, "chan")
    attended = attend(at, qkv, bias, bias_other, penalty, width)
    attended = exchange(attended, "chan")

    homolog_after_update, left, right = sides(
        attended,
        gate,
        homolog_stack,
        homolog_occupancy,
        focus_exit_coefficients,
        tensor_entry_coefficients,
    )
    right = ring_gather(right)
    right_other = swap(right)
    members = 2 * planes
    packed_rows = residues * side // 128
    steps = chan * packed_rows // members
    left = exchange(left, "chan")
    left = jnp.concatenate(
        [
            left[:, :packed_rows].reshape(members, steps, 128),
            jnp.repeat(left[:, packed_rows : packed_rows + 8], members // chan, axis=0),
        ],
        axis=1,
    )
    left = exchange(left, BRANCH_ROW)
    left = repeated(left[:, : steps + 1].transpose(1, 0, 2), chan)
    left = exchange(left, "chan")
    mid, left_tri, right_tri = outer(
        at,
        left,
        right,
        right_other,
        couple_tensor,
        live_rows[:, None] * live_cols[None, :],
        tensor_exit_coefficients,
        trio_entry_coefficients,
    )
    operands = jnp.stack([left_tri, right_tri]).transpose(2, 0, 1, 3)
    operands = exchange(operands, CHIPS)
    grid = (planes, chan, pair_rows, pair_cols)
    left_tri, right_tri = operands[:, 0].reshape(grid), operands[:, 1].reshape(grid)
    product = triangle(me, left_tri, right_tri, swap(right_tri))
    product = exchange(product.reshape(pair_width, pair_rows, pair_cols), CHIPS)
    gate = switch(mid, trio_exit_switch)
    pair_result = finish(product, mid, gate, trio_exit_coefficients)
    return (homolog_after_update, pair_result)


def solution(mesh):
    torus = Mesh(
        mesh.devices.reshape(mesh.shape["branch"], 8, 2, mesh.shape["chan"]),
        ("branch", "row_0", "row_1", "chan"),
    )

    return jax.shard_map(
        shards,
        mesh=torus,
        in_specs=(
            P(BRANCH_ROW, "chan", None),
            P(BRANCH_ROW, "chan", None),
            P(),
            P(BRANCH_ROW, "chan"),
            *(P() for _ in range(8)),
        ),
        out_specs=(P(BRANCH_ROW, "chan", None), P(BRANCH_ROW, "chan", None)),
        check_vma=False,
    )
```

```python
import functools

import jax
import jax.numpy as jnp
from jax import lax
from jax.experimental import pallas as pl
from jax.experimental.pallas import tpu as pltpu
from jax.sharding import Mesh
from jax.sharding import PartitionSpec as P


BRANCH_ROW = ("branch", "row_0", "row_1")
CHIPS = ("branch", "row_0", "chan")
SWAP = ((0, 1), (1, 0))
EPSILON = 1e-05
MASKED = 1000000000.0
LOG2E = 1.4426950408889634
BF16 = jnp.bfloat16
F32 = jnp.float32


def params(mebibytes):
    return pltpu.CompilerParams(
        dimension_semantics=("arbitrary",), vmem_limit_bytes=mebibytes * 1024 * 1024
    )


def dot(a, b, dims):
    return lax.dot_general(a, b, ((dims[:1], dims[1:]), ((), ())), preferred_element_type=F32)


def standardize(values, axis):
    values = values.astype(F32)
    centered = values - jnp.mean(values, axis=axis, keepdims=True)
    spread = jnp.mean(centered * centered, axis=axis, keepdims=True)
    return centered * lax.rsqrt(spread + EPSILON)


def sigmoid(x):
    return 1.0 / (1.0 + jnp.exp(-x))


def whole(shape):
    return pl.BlockSpec(shape, lambda *_: (0,) * len(shape))


def bias_kernel(x_ref, w_ref, out_ref, hold_ref):
    step = pl.program_id(0)
    rows, lanes, channels = x_ref.shape
    heads, pair_rows, _ = out_ref.shape
    normed = standardize(x_ref[...].reshape(rows * lanes, channels), -1).astype(BF16)
    bias = dot(w_ref[...], normed, (1, 1))
    for i in range(rows):
        hold_ref[pl.ds(step * rows + i, heads, stride=pair_rows), :] = bias[
            :, i * lanes : (i + 1) * lanes
        ]

    @pl.when(step == pl.num_programs(0) - 1)
    def _():
        out_ref[...] = hold_ref[...].astype(BF16).reshape(heads, pair_rows, lanes)


def pair_bias(couple, weights):
    pair_rows, lanes, channels = couple.shape
    heads = weights.shape[1]
    rows = 8
    return pl.pallas_call(
        bias_kernel,
        grid=(pair_rows // rows,),
        in_specs=[
            pl.BlockSpec((rows, lanes, channels), lambda t: (t, 0, 0)),
            whole((heads, channels)),
        ],
        out_specs=whole((heads, pair_rows, lanes)),
        out_shape=jax.ShapeDtypeStruct((heads, pair_rows, lanes), BF16),
        scratch_shapes=[pltpu.VMEM((heads * pair_rows, lanes), F32)],
        compiler_params=params(60),
        name="pair_bias",
    )(couple, weights.T)


def project_kernel(heads, width, x_ref, w_ref, qkv_ref, gate_ref):
    entries, residues, features = x_ref.shape
    normed = standardize(x_ref[...].reshape(entries * residues, features), -1).astype(BF16)
    packed = dot(w_ref[...], normed, (1, 1)).astype(BF16)
    for s in range(entries):
        at = slice(s * residues, (s + 1) * residues)
        for h in range(heads):
            base = h * 4 * width
            qkv_ref[h, s] = packed[base : base + 3 * width, at]
            gate_ref[s, h * width : (h + 1) * width] = packed[
                base + 3 * width : base + 4 * width, at
            ]


def project_msa(stack, weights, heads):
    entries, residues, features = stack.shape
    width = features // heads
    take = 2
    return pl.pallas_call(
        functools.partial(project_kernel, heads, width),
        grid=(entries // take,),
        in_specs=[
            pl.BlockSpec((take, residues, features), lambda s: (s, 0, 0)),
            whole((4 * features, features)),
        ],
        out_specs=[
            pl.BlockSpec((heads, take, 3 * width, residues), lambda s: (0, s, 0, 0)),
            pl.BlockSpec((take, features, residues), lambda s: (s, 0, 0)),
        ],
        out_shape=[
            jax.ShapeDtypeStruct((heads, entries, 3 * width, residues), BF16),
            jax.ShapeDtypeStruct((entries, features, residues), BF16),
        ],
        compiler_params=params(16),
        name="project_msa",
    )(stack, weights.T)


def attend_kernel(width, at_ref, qkv_ref, mine_ref, other_ref, pen_ref, out_ref, bias_ref, value_ref):
    block = pl.program_id(0)
    columns, entries = qkv_ref.shape[0], qkv_ref.shape[1]
    lanes = qkv_ref.shape[3]
    take = out_ref.shape[0]
    length, _, _, tile, _ = mine_ref.shape
    first = at_ref[0] == 0

    @pl.when(block == 0)
    def _():
        ones = jnp.ones((lanes - width, lanes), F32)

        @pl.loop(0, entries)
        def _(s):
            for j in range(columns):
                part = jnp.concatenate([qkv_ref[j, s, 2 * width :].astype(F32), ones], axis=0)
                value_ref[s, j * lanes : (j + 1) * lanes] = part.T.astype(BF16)

    planes = take * lanes // (2 * tile)

    @pl.loop(0, planes)
    def _(q):
        plane = block * planes + q
        place = ring_place((plane + 2 * length - at_ref[2]) % length, length)
        side = jnp.bitwise_xor(plane // length, at_ref[1])
        upper = pl.ds(pl.multiple_of(q * 2 * tile, tile), tile)
        lower = pl.ds(pl.multiple_of(q * 2 * tile + tile, tile), tile)
        for j in range(columns):
            a = mine_ref[place, side, j].astype(F32)
            b = other_ref[place, side, j].astype(F32)
            at = slice(j * lanes, (j + 1) * lanes)
            pen = pen_ref[:, at]
            bias_ref[upper, at] = (jnp.where(first, a, b) + pen) * LOG2E
            bias_ref[lower, at] = (jnp.where(first, b, a) + pen) * LOG2E

    scale = width ** (-0.5) * LOG2E
    for s in range(entries):
        query = jnp.concatenate([qkv_ref[block * take + t, s, 0:width] for t in range(take)], axis=1)
        query = (query.astype(F32) * scale).T.astype(BF16)
        keys = jnp.concatenate([qkv_ref[j, s, width : 2 * width] for j in range(columns)], axis=1)
        logits = dot(query, keys, (1, 0)) + bias_ref[...]
        top = jnp.max(logits, axis=1, keepdims=True)
        weights = jnp.exp2(logits - top).astype(BF16)
        blended = dot(weights, value_ref[s], (1, 0))
        for t in range(take):
            part = blended[t * lanes : (t + 1) * lanes].T
            out_ref[t, s] = (part[:width] * (1.0 / part[width : width + 1])).astype(BF16)


def attend(at, qkv, mine, other, pen, width):
    columns, entries, _, lanes = qkv.shape
    take = 4
    return pl.pallas_call(
        functools.partial(attend_kernel, width),
        grid_spec=pltpu.PrefetchScalarGridSpec(
            num_scalar_prefetch=1,
            grid=(columns // take,),
            in_specs=[whole(qkv.shape), whole(mine.shape), whole(other.shape), whole(pen.shape)],
            out_specs=pl.BlockSpec((take, entries, width, lanes), lambda b, at: (b, 0, 0, 0)),
            scratch_shapes=[
                pltpu.VMEM((take * lanes, columns * lanes), F32),
                pltpu.VMEM((entries, columns * lanes, lanes), BF16),
            ],
        ),
        out_shape=jax.ShapeDtypeStruct((columns, entries, width, lanes), BF16),
        compiler_params=params(48),
        name="attend",
    )(at, qkv, mine, other, pen)


def sides_kernel(
    side, att_ref, gate_ref, stack_ref, mask_ref, wo_ref, wl_ref, wr_ref, out_ref, left_ref, right_ref, hold_ref
):
    step = pl.program_id(0)
    take, residues, features = stack_ref.shape
    gated = jnp.concatenate(
        [
            (
                att_ref[:, s].astype(F32).reshape(-1, residues) * sigmoid(gate_ref[s].astype(F32))
            ).astype(BF16)
            for s in range(take)
        ],
        axis=1,
    )
    stack = stack_ref[...].astype(F32).reshape(take * residues, features)
    updated = (stack + dot(gated, wo_ref[...], (0, 0))).astype(BF16)
    out_ref[...] = updated.reshape(take, residues, features)
    normed = standardize(updated, -1).astype(BF16)
    right = dot(wr_ref[...], normed, (1, 1))
    group = 128 // side
    spread = dot(normed, wl_ref[...], (1, 0))
    rows = lax.broadcasted_iota(jnp.int32, spread.shape, 0)
    lanes = lax.broadcasted_iota(jnp.int32, spread.shape, 1)
    spread = jnp.where(rows % group == lanes // side, spread, 0.0).astype(BF16)
    to = lax.broadcasted_iota(jnp.int32, (residues // group, residues), 0)
    of = lax.broadcasted_iota(jnp.int32, (residues // group, residues), 1)
    gather = jnp.where(of // group == to, 1.0, 0.0)
    tail = lax.broadcasted_iota(jnp.int32, (16, residues), 0)
    for s in range(take):
        mask = mask_ref[s]
        at = slice(s * residues, (s + 1) * residues)
        hold_ref[pl.ds(step * take + s, side, stride=8), :] = right[:, at] * mask
        hold_ref[pl.ds(side * 8 + step * take + s, 1), :] = mask
        left = dot((gather * mask).astype(BF16), spread[at], (1, 0))
        left_ref[s, 0 : residues // group] = left.astype(BF16)
        left_ref[s, residues // group :] = jnp.where(tail == 0, mask, 0.0).astype(BF16)

    @pl.when(step == pl.num_programs(0) - 1)
    def _():
        right_ref[...] = hold_ref[...].astype(BF16)


def sides(attended, gate, stack, mask, w_out, w_sides):
    entries, residues, features = stack.shape
    heads, _, width, _ = attended.shape
    side = w_sides.shape[1] // 2
    group = 128 // side
    rows = residues // group + 16
    take = 4
    return pl.pallas_call(
        functools.partial(sides_kernel, side),
        grid=(entries // take,),
        in_specs=[
            pl.BlockSpec((heads, take, width, residues), lambda s: (0, s, 0, 0)),
            pl.BlockSpec((take, features, residues), lambda s: (s, 0, 0)),
            pl.BlockSpec((take, residues, features), lambda s: (s, 0, 0)),
            pl.BlockSpec((take, 1, residues), lambda s: (s, 0, 0)),
            whole(w_out.shape),
            whole((features, 128)),
            whole((side, features)),
        ],
        out_specs=[
            pl.BlockSpec((take, residues, features), lambda s: (s, 0, 0)),
            pl.BlockSpec((take, rows, 128), lambda s: (s, 0, 0)),
            whole(((side + 1) * 8, residues)),
        ],
        out_shape=[
            jax.ShapeDtypeStruct(stack.shape, BF16),
            jax.ShapeDtypeStruct((entries, rows, 128), BF16),
            jax.ShapeDtypeStruct(((side + 1) * 8, residues), BF16),
        ],
        scratch_shapes=[pltpu.VMEM(((side + 1) * 8, residues), F32)],
        compiler_params=params(16),
        name="sides",
    )(
        attended,
        gate,
        stack,
        mask[:, None, :].astype(F32),
        w_out,
        jnp.tile(w_sides[:, :side], (1, group)),
        w_sides[:, side:].T,
    )


OUTER_CHUNKS = 2


def outer_kernel(
    side, at_ref, left_ref, mine_ref, other_ref, couple_ref, live_ref, we_ref, wt_ref,
    mid_ref, l_ref, r_ref, right_ref, rmask_ref, rows_ref, x_ref, update_ref, count_ref,
):
    step = pl.program_id(0)
    rows, lanes = couple_ref.shape[0], couple_ref.shape[1]
    channels = couple_ref.shape[2]
    pair_rows = live_ref.shape[0]
    entries = rmask_ref.shape[0]

    @pl.when(step == 0)
    def _():
        length, branches = mine_ref.shape[0], mine_ref.shape[1]

        @pl.loop(0, branches * length)
        def _(plane):
            place = ring_place((plane + branches * length - at_ref[2]) % length, length)
            which = jnp.bitwise_xor(plane // length, at_ref[1])
            at = pl.ds(pl.multiple_of(plane * 16, 16), 16)
            for d in range(side + 1):
                pair = [ref[place, which, d * 8 : (d + 1) * 8] for ref in (mine_ref, other_ref)]
                pair = jnp.concatenate(pair, axis=0)
                if d < side:
                    right_ref[d // 2, at, d % 2 * lanes : (d % 2 + 1) * lanes] = pair
                else:
                    rmask_ref[at, :] = pair

        columns, tiles, members, _ = left_ref.shape
        given = lax.broadcasted_iota(jnp.int32, (entries, entries), 0)
        wanted = lax.broadcasted_iota(jnp.int32, (entries, entries), 1)
        member = jnp.bitwise_xor(given % members, at_ref[0])
        order = jnp.where(member * columns + given // members == wanted, 1.0, 0.0).astype(BF16)
        for t in range(tiles):
            rows_in = jnp.concatenate([left_ref[c, t] for c in range(columns)], axis=0)
            turned = dot(rows_in, order, (0, 0)).astype(BF16)
            if t < tiles - 1:
                rows_ref[t * 128 : (t + 1) * 128] = turned
            else:
                count_ref[...] = 1.0 / (dot(turned, rmask_ref[...], (1, 0)) + 1.0)

    @pl.when(step < OUTER_CHUNKS)
    def _():
        part = side // OUTER_CHUNKS
        for k in range(0, part, 2):
            sums = dot(rows_ref[...], right_ref[step * (part // 2) + k // 2], (1, 0)).astype(BF16)
            for i in range(pair_rows):
                for e in range(2):
                    x_ref[(k + e) * side : (k + e + 1) * side, i * lanes : (i + 1) * lanes] = sums[
                        i * side : (i + 1) * side, e * lanes : (e + 1) * lanes
                    ]
        added = dot(we_ref[step], x_ref[...], (1, 0))

        @pl.when(step == 0)
        def _():
            update_ref[...] = added

        @pl.when(step > 0)
        def _():
            update_ref[...] += added

    @pl.when(step >= OUTER_CHUNKS)
    def _():
        first = (step - OUTER_CHUNKS) * rows
        normed = []
        for i in range(rows):
            over = count_ref[pl.ds(at_ref[3] * pair_rows + first + i, 1), :]
            update = update_ref[:, pl.ds(pl.multiple_of((first + i) * lanes, lanes), lanes)]
            mid = couple_ref[i].astype(F32).T + update * over
            mid_ref[i] = mid
            normed.append(standardize(mid, 0).astype(BF16))
        normed = jnp.concatenate(normed, axis=1)
        for part, ref in ((0, l_ref), (2, r_ref)):
            gate = dot(wt_ref[part * channels : (part + 1) * channels], normed, (1, 0))
            value = dot(wt_ref[(part + 1) * channels : (part + 2) * channels], normed, (1, 0))
            both = sigmoid(gate) * value
            for i in range(rows):
                live = live_ref[pl.ds(first + i, 1), :]
                ref[i] = (both[:, i * lanes : (i + 1) * lanes] * live).astype(BF16)


def outer(at, left, mine, other, couple, live, w_exit, w_tri):
    entries = left.shape[0] * left.shape[2]
    pair_rows, lanes, channels = couple.shape
    rows = 8
    side = mine.shape[2] // 8 - 1
    move = lambda t, at: (jnp.maximum(t - OUTER_CHUNKS, 0), 0, 0)
    tile = pl.BlockSpec((rows, channels, lanes), move)
    depth = side * side // OUTER_CHUNKS
    w_exit = w_exit.reshape(side, side, channels).transpose(1, 0, 2)
    w_exit = w_exit.reshape(OUTER_CHUNKS, depth, channels).transpose(0, 2, 1)
    return pl.pallas_call(
        functools.partial(outer_kernel, side),
        grid_spec=pltpu.PrefetchScalarGridSpec(
            num_scalar_prefetch=1,
            grid=(OUTER_CHUNKS + pair_rows // rows,),
            in_specs=[
                whole(left.shape),
                whole(mine.shape),
                whole(other.shape),
                pl.BlockSpec((rows, lanes, channels), move),
                whole(live.shape),
                whole(w_exit.shape),
                whole((4 * channels, channels)),
            ],
            out_specs=[tile, tile, tile],
            scratch_shapes=[
                pltpu.VMEM((side // 2, entries, 2 * lanes), BF16),
                pltpu.VMEM((entries, lanes), BF16),
                pltpu.VMEM((pair_rows * side, entries), BF16),
                pltpu.VMEM((depth, pair_rows * lanes), BF16),
                pltpu.VMEM((channels, pair_rows * lanes), F32),
                pltpu.VMEM((128, lanes), F32),
            ],
        ),
        out_shape=[
            jax.ShapeDtypeStruct((pair_rows, channels, lanes), F32),
            jax.ShapeDtypeStruct((pair_rows, channels, lanes), BF16),
            jax.ShapeDtypeStruct((pair_rows, channels, lanes), BF16),
        ],
        compiler_params=params(60),
        name="outer",
    )(at, left, mine, other, couple, live, w_exit, w_tri.T)


def triangle_kernel(me_ref, l_ref, mine_ref, other_ref, out_ref):
    planes, columns, tile, lanes = l_ref.shape
    first = me_ref[0] == 0
    joined = lambda ref, p: jnp.concatenate([ref[p, k] for k in range(columns)], axis=1)
    rights = []
    for p in range(mine_ref.shape[0]):
        a, b = joined(mine_ref, p), joined(other_ref, p)
        rights += [jnp.where(first, a, b), jnp.where(first, b, a)]
    right = jnp.concatenate(rights, axis=0)
    per = lanes // (2 * tile)
    for p in range(0, planes, 4):
        left = jnp.concatenate([joined(l_ref, p + q) for q in range(4)], axis=0)
        product = dot(left, right, (1, 1)).astype(BF16)
        for q in range(4):
            for n in range(mine_ref.shape[0] // per):
                out_ref[p + q, n] = product[
                    q * tile : (q + 1) * tile, n * lanes : (n + 1) * lanes
                ]


def triangle(me, left, mine, other):
    planes, columns, tile, lanes = left.shape
    per = lanes // (2 * tile)
    take = 2
    spec = pl.BlockSpec((per * take, columns, tile, lanes), lambda n, me: (n, 0, 0, 0))
    return pl.pallas_call(
        triangle_kernel,
        grid_spec=pltpu.PrefetchScalarGridSpec(
            num_scalar_prefetch=1,
            grid=(columns // take,),
            in_specs=[whole(left.shape), spec, spec],
            out_specs=pl.BlockSpec((planes, take, tile, lanes), lambda n, me: (0, n, 0, 0)),
        ),
        out_shape=jax.ShapeDtypeStruct(left.shape, BF16),
        compiler_params=params(20),
        name="triangle",
    )(me, left, mine, other)


def switch_kernel(mid_ref, ws_ref, gate_ref):
    rows, _, lanes = mid_ref.shape
    normed = [standardize(mid_ref[i], 0).astype(BF16) for i in range(rows)]
    gate = sigmoid(dot(ws_ref[...], jnp.concatenate(normed, axis=1), (1, 0)))
    for i in range(rows):
        gate_ref[i] = gate[:, i * lanes : (i + 1) * lanes]


def switch(mid, w_switch):
    pair_rows, channels, lanes = mid.shape
    tile = pl.BlockSpec((2, channels, lanes), lambda t: (t, 0, 0))
    return pl.pallas_call(
        switch_kernel,
        grid=(pair_rows // 2,),
        in_specs=[tile, whole(w_switch.shape)],
        out_specs=tile,
        out_shape=jax.ShapeDtypeStruct(mid.shape, F32),
        compiler_params=params(16),
        name="switch",
    )(mid, w_switch.T)


def finish_kernel(prod_ref, mid_ref, gate_ref, wo_ref, out_ref, mixed_ref):
    step = pl.program_id(0)
    channels, pair_rows, lanes = prod_ref.shape
    rows = mid_ref.shape[0]

    @pl.when(step == 0)
    def _():
        zero = jnp.zeros((pair_rows, lanes), F32)
        take = 16

        def add(k, total):
            for c in range(take):
                total = total + prod_ref[k * take + c].astype(F32)
            return total

        mean = lax.fori_loop(0, channels // take, add, zero) / channels

        def add_square(k, total):
            for c in range(take):
                centered = prod_ref[k * take + c].astype(F32) - mean
                total = total + centered * centered
            return total

        spread = lax.fori_loop(0, channels // take, add_square, zero) / channels
        inverse = lax.rsqrt(spread + EPSILON)

        @pl.loop(0, channels // take)
        def _(k):
            for c in range(take):
                row = pl.multiple_of((k * take + c) * pair_rows, pair_rows)
                mixed_ref[pl.ds(row, pair_rows), :] = (
                    prod_ref[k * take + c].astype(F32) - mean
                ) * inverse

    mixed = [
        mixed_ref[pl.ds(step * rows + i, channels, stride=pair_rows), :].astype(BF16)
        for i in range(rows)
    ]
    update = dot(wo_ref[...], jnp.concatenate(mixed, axis=1), (1, 0))
    for i in range(rows):
        result = mid_ref[i] + update[:, i * lanes : (i + 1) * lanes] * gate_ref[i]
        out_ref[i] = result.T.astype(BF16)


def finish(product, mid, gate, w_out):
    channels, pair_rows, lanes = product.shape
    rows = 8
    tile = pl.BlockSpec((rows, channels, lanes), lambda t: (t, 0, 0))
    return pl.pallas_call(
        finish_kernel,
        grid=(pair_rows // rows,),
        in_specs=[whole(product.shape), tile, tile, whole(w_out.shape)],
        out_specs=pl.BlockSpec((rows, lanes, channels), lambda t: (t, 0, 0)),
        out_shape=jax.ShapeDtypeStruct((pair_rows, lanes, channels), BF16),
        scratch_shapes=[pltpu.VMEM((channels * pair_rows, lanes), F32)],
        compiler_params=params(24),
        name="finish",
    )(product, mid, gate, w_out.T)


def swap(x):
    return lax.ppermute(x, "row_1", SWAP)


def exchange(x, axes):
    return lax.all_to_all(x, axes, 0, 0, tiled=True)


def ring_gather(x):
    n = lax.axis_size("row_0")

    def shift(y, by):
        return lax.ppermute(y, "row_0", tuple((k, (k + by) % n) for k in range(n)))

    across = lax.ppermute(x, "branch", SWAP)
    pair = jnp.stack([x, across])
    above, below, above_2, below_2 = (shift(pair, by) for by in (1, -1, 2, -2))
    above_3, below_3 = shift(above_2, 1), shift(below_2, -1)
    last = [shift(above_2[:1], 2), shift(below_2[1:], -2)]
    return jnp.stack([pair, above, below, above_2, below_2, above_3, below_3, jnp.concatenate(last)])


def ring_place(ahead, n):
    return jnp.where(ahead <= n // 2, jnp.maximum(2 * ahead - (ahead == n // 2), 0), 2 * (n - ahead) - 1)


def repeated(x, n):
    return jnp.broadcast_to(x[None], (n, *x.shape))


def shards(
    homolog_stack,
    couple_tensor,
    amino_occupancy,
    homolog_occupancy,
    focus_entry_coefficients,
    couple_offset_coefficients,
    focus_exit_coefficients,
    tensor_entry_coefficients,
    tensor_exit_coefficients,
    trio_entry_coefficients,
    trio_exit_switch,
    trio_exit_coefficients,
):
    _, residues, features = homolog_stack.shape
    pair_rows, pair_cols, pair_width = couple_tensor.shape
    heads = couple_offset_coefficients.shape[1]
    width = features // heads
    side = tensor_entry_coefficients.shape[1] // 2
    planes = lax.axis_size("branch") * lax.axis_size("row_0")
    chan = lax.axis_size("chan")
    core = lax.axis_index("row_1").astype(jnp.int32)
    row = lax.axis_index(BRANCH_ROW).astype(jnp.int32)
    place = [core, lax.axis_index("branch"), lax.axis_index("row_0"), row % 4]
    at = jnp.stack([p.astype(jnp.int32) for p in place])
    me = core.reshape(1)
    live = amino_occupancy.astype(F32)
    live_rows = lax.dynamic_slice_in_dim(live, row * pair_rows, pair_rows)
    live_cols = lax.dynamic_slice_in_dim(live, lax.axis_index("chan") * pair_cols, pair_cols)
    penalty = ((live - 1.0) * MASKED)[None, :]

    bias = pair_bias(couple_tensor, couple_offset_coefficients)
    bias = exchange(bias, "chan")
    bias = ring_gather(bias)
    bias_other = swap(bias)

    qkv, gate = project_msa(homolog_stack, focus_entry_coefficients, heads)
    qkv = exchange(qkv, "chan")
    attended = attend(at, qkv, bias, bias_other, penalty, width)
    attended = exchange(attended, "chan")

    homolog_after_update, left, right = sides(
        attended,
        gate,
        homolog_stack,
        homolog_occupancy,
        focus_exit_coefficients,
        tensor_entry_coefficients,
    )
    right = ring_gather(right)
    right_other = swap(right)
    members = 2 * planes
    packed_rows = residues * side // 128
    steps = chan * packed_rows // members
    left = exchange(left, "chan")
    left = jnp.concatenate(
        [
            left[:, :packed_rows].reshape(members, steps, 128),
            jnp.repeat(left[:, packed_rows : packed_rows + 8], members // chan, axis=0),
        ],
        axis=1,
    )
    left = exchange(left, BRANCH_ROW)
    left = repeated(left[:, : steps + 1].transpose(1, 0, 2), chan)
    left = exchange(left, "chan")
    mid, left_tri, right_tri = outer(
        at,
        left,
        right,
        right_other,
        couple_tensor,
        live_rows[:, None] * live_cols[None, :],
        tensor_exit_coefficients,
        trio_entry_coefficients,
    )
    operands = jnp.stack([left_tri, right_tri]).transpose(2, 0, 1, 3)
    operands = exchange(operands, CHIPS)
    grid = (planes, chan, pair_rows, pair_cols)
    left_tri, right_tri = operands[:, 0].reshape(grid), operands[:, 1].reshape(grid)
    product = triangle(me, left_tri, right_tri, swap(right_tri))
    product = exchange(product.reshape(pair_width, pair_rows, pair_cols), CHIPS)
    gate = switch(mid, trio_exit_switch)
    pair_result = finish(product, mid, gate, trio_exit_coefficients)
    return (homolog_after_update, pair_result)


def solution(mesh):
    torus = Mesh(
        mesh.devices.reshape(mesh.shape["branch"], 8, 2, mesh.shape["chan"]),
        ("branch", "row_0", "row_1", "chan"),
    )

    return jax.shard_map(
        shards,
        mesh=torus,
        in_specs=(
            P(BRANCH_ROW, "chan", None),
            P(BRANCH_ROW, "chan", None),
            P(),
            P(BRANCH_ROW, "chan"),
            *(P() for _ in range(8)),
        ),
        out_specs=(P(BRANCH_ROW, "chan", None), P(BRANCH_ROW, "chan", None)),
        check_vma=False,
    )
```

```python
import functools

import jax
import jax.numpy as jnp
from jax import lax
from jax.experimental import pallas as pl
from jax.experimental.layout import Layout, with_layout_constraint
from jax.experimental.pallas import tpu as pltpu
from jax.sharding import Mesh
from jax.sharding import PartitionSpec as P


BRANCH_ROW = ("branch", "row_0", "row_1")
CHIPS = ("branch", "row_0", "chan")
SWAP = ((0, 1), (1, 0))
EPSILON = 1e-05
MASKED = 1000000000.0
LOG2E = 1.4426950408889634
BF16 = jnp.bfloat16
F32 = jnp.float32


def params(mebibytes):
    return pltpu.CompilerParams(
        dimension_semantics=("arbitrary",), vmem_limit_bytes=mebibytes * 1024 * 1024
    )


def dot(a, b, dims):
    return lax.dot_general(a, b, ((dims[:1], dims[1:]), ((), ())), preferred_element_type=F32)


def standardize(values, axis):
    values = values.astype(F32)
    centered = values - jnp.mean(values, axis=axis, keepdims=True)
    spread = jnp.mean(centered * centered, axis=axis, keepdims=True)
    return centered * lax.rsqrt(spread + EPSILON)


def sigmoid(x):
    return 1.0 / (1.0 + jnp.exp(-x))


def whole(shape):
    return pl.BlockSpec(shape, lambda *_: (0,) * len(shape))


def bias_kernel(x_ref, w_ref, out_ref, hold_ref):
    step = pl.program_id(0)
    rows, lanes, channels = x_ref.shape
    heads, pair_rows, _ = out_ref.shape
    normed = standardize(x_ref[...].reshape(rows * lanes, channels), -1).astype(BF16)
    bias = dot(w_ref[...], normed, (1, 1))
    for i in range(rows):
        hold_ref[pl.ds(step * rows + i, heads, stride=pair_rows), :] = bias[
            :, i * lanes : (i + 1) * lanes
        ]

    @pl.when(step == pl.num_programs(0) - 1)
    def _():
        out_ref[...] = hold_ref[...].astype(BF16).reshape(heads, pair_rows, lanes)


def pair_bias(couple, weights):
    pair_rows, lanes, channels = couple.shape
    heads = weights.shape[1]
    rows = 8
    return pl.pallas_call(
        bias_kernel,
        grid=(pair_rows // rows,),
        in_specs=[
            pl.BlockSpec((rows, lanes, channels), lambda t: (t, 0, 0)),
            whole((heads, channels)),
        ],
        out_specs=whole((heads, pair_rows, lanes)),
        out_shape=jax.ShapeDtypeStruct((heads, pair_rows, lanes), BF16),
        scratch_shapes=[pltpu.VMEM((heads * pair_rows, lanes), F32)],
        compiler_params=params(60),
        name="pair_bias",
    )(couple, weights.T)


def project_kernel(heads, width, x_ref, w_ref, qkv_ref, gate_ref):
    entries, residues, features = x_ref.shape
    normed = standardize(x_ref[...].reshape(entries * residues, features), -1).astype(BF16)
    packed = dot(w_ref[...], normed, (1, 1)).astype(BF16)
    for s in range(entries):
        at = slice(s * residues, (s + 1) * residues)
        for h in range(heads):
            base = h * 4 * width
            qkv_ref[h, s] = packed[base : base + 3 * width, at]
            gate_ref[s, h * width : (h + 1) * width] = packed[
                base + 3 * width : base + 4 * width, at
            ]


def project_msa(stack, weights, heads):
    entries, residues, features = stack.shape
    width = features // heads
    take = 2
    return pl.pallas_call(
        functools.partial(project_kernel, heads, width),
        grid=(entries // take,),
        in_specs=[
            pl.BlockSpec((take, residues, features), lambda s: (s, 0, 0)),
            whole((4 * features, features)),
        ],
        out_specs=[
            pl.BlockSpec((heads, take, 3 * width, residues), lambda s: (0, s, 0, 0)),
            pl.BlockSpec((take, features, residues), lambda s: (s, 0, 0)),
        ],
        out_shape=[
            jax.ShapeDtypeStruct((heads, entries, 3 * width, residues), BF16),
            jax.ShapeDtypeStruct((entries, features, residues), BF16),
        ],
        compiler_params=params(16),
        name="project_msa",
    )(stack, weights.T)


def attend_kernel(width, at_ref, qkv_ref, mine_ref, other_ref, pen_ref, out_ref, bias_ref, value_ref):
    block = pl.program_id(0)
    columns, entries = qkv_ref.shape[0], qkv_ref.shape[1]
    lanes = qkv_ref.shape[3]
    take = out_ref.shape[0]
    length, _, _, tile, _ = mine_ref.shape
    first = at_ref[0] == 0

    @pl.when(block == 0)
    def _():
        ones = jnp.ones((lanes - width, lanes), F32)

        @pl.loop(0, entries)
        def _(s):
            for j in range(columns):
                part = jnp.concatenate([qkv_ref[j, s, 2 * width :].astype(F32), ones], axis=0)
                value_ref[s, j * lanes : (j + 1) * lanes] = part.T.astype(BF16)

    planes = take * lanes // (2 * tile)

    @pl.loop(0, planes)
    def _(q):
        plane = block * planes + q
        place = ring_place((plane + 2 * length - at_ref[2]) % length, length)
        side = jnp.bitwise_xor(plane // length, at_ref[1])
        upper = pl.ds(pl.multiple_of(q * 2 * tile, tile), tile)
        lower = pl.ds(pl.multiple_of(q * 2 * tile + tile, tile), tile)
        for j in range(columns):
            a = mine_ref[place, side, j].astype(F32)
            b = other_ref[place, side, j].astype(F32)
            at = slice(j * lanes, (j + 1) * lanes)
            pen = pen_ref[:, at]
            bias_ref[upper, at] = (jnp.where(first, a, b) + pen) * LOG2E
            bias_ref[lower, at] = (jnp.where(first, b, a) + pen) * LOG2E

    scale = width ** (-0.5) * LOG2E
    for s in range(entries):
        query = jnp.concatenate([qkv_ref[block * take + t, s, 0:width] for t in range(take)], axis=1)
        query = (query.astype(F32) * scale).T.astype(BF16)
        keys = jnp.concatenate([qkv_ref[j, s, width : 2 * width] for j in range(columns)], axis=1)
        logits = dot(query, keys, (1, 0)) + bias_ref[...]
        top = jnp.max(logits, axis=1, keepdims=True)
        weights = jnp.exp2(logits - top).astype(BF16)
        blended = dot(weights, value_ref[s], (1, 0))
        for t in range(take):
            part = blended[t * lanes : (t + 1) * lanes].T
            out_ref[t, s] = (part[:width] * (1.0 / part[width : width + 1])).astype(BF16)


def attend(at, qkv, mine, other, pen, width):
    columns, entries, _, lanes = qkv.shape
    take = 4
    return pl.pallas_call(
        functools.partial(attend_kernel, width),
        grid_spec=pltpu.PrefetchScalarGridSpec(
            num_scalar_prefetch=1,
            grid=(columns // take,),
            in_specs=[whole(qkv.shape), whole(mine.shape), whole(other.shape), whole(pen.shape)],
            out_specs=pl.BlockSpec((take, entries, width, lanes), lambda b, at: (b, 0, 0, 0)),
            scratch_shapes=[
                pltpu.VMEM((take * lanes, columns * lanes), F32),
                pltpu.VMEM((entries, columns * lanes, lanes), BF16),
            ],
        ),
        out_shape=jax.ShapeDtypeStruct((columns, entries, width, lanes), BF16),
        compiler_params=params(48),
        name="attend",
    )(at, qkv, mine, other, pen)


def sides_kernel(
    side, att_ref, gate_ref, stack_ref, mask_ref, wo_ref, wl_ref, wr_ref, out_ref, left_ref, right_ref, hold_ref
):
    step = pl.program_id(0)
    take, residues, features = stack_ref.shape
    gated = jnp.concatenate(
        [
            (
                att_ref[:, s].astype(F32).reshape(-1, residues) * sigmoid(gate_ref[s].astype(F32))
            ).astype(BF16)
            for s in range(take)
        ],
        axis=1,
    )
    stack = stack_ref[...].astype(F32).reshape(take * residues, features)
    updated = (stack + dot(gated, wo_ref[...], (0, 0))).astype(BF16)
    out_ref[...] = updated.reshape(take, residues, features)
    normed = standardize(updated, -1).astype(BF16)
    right = dot(wr_ref[...], normed, (1, 1))
    group = 128 // side
    spread = dot(normed, wl_ref[...], (1, 0))
    rows = lax.broadcasted_iota(jnp.int32, spread.shape, 0)
    lanes = lax.broadcasted_iota(jnp.int32, spread.shape, 1)
    spread = jnp.where(rows % group == lanes // side, spread, 0.0).astype(BF16)
    to = lax.broadcasted_iota(jnp.int32, (residues // group, residues), 0)
    of = lax.broadcasted_iota(jnp.int32, (residues // group, residues), 1)
    gather = jnp.where(of // group == to, 1.0, 0.0)
    tail = lax.broadcasted_iota(jnp.int32, (16, residues), 0)
    for s in range(take):
        mask = mask_ref[s]
        at = slice(s * residues, (s + 1) * residues)
        hold_ref[pl.ds(step * take + s, side, stride=8), :] = right[:, at] * mask
        hold_ref[pl.ds(side * 8 + step * take + s, 1), :] = mask
        left = dot((gather * mask).astype(BF16), spread[at], (1, 0))
        left_ref[s, 0 : residues // group] = left.astype(BF16)
        left_ref[s, residues // group :] = jnp.where(tail == 0, mask, 0.0).astype(BF16)

    @pl.when(step == pl.num_programs(0) - 1)
    def _():
        right_ref[...] = hold_ref[...].astype(BF16)


def sides(attended, gate, stack, mask, w_out, w_sides):
    entries, residues, features = stack.shape
    heads, _, width, _ = attended.shape
    side = w_sides.shape[1] // 2
    group = 128 // side
    rows = residues // group + 16
    take = 4
    return pl.pallas_call(
        functools.partial(sides_kernel, side),
        grid=(entries // take,),
        in_specs=[
            pl.BlockSpec((heads, take, width, residues), lambda s: (0, s, 0, 0)),
            pl.BlockSpec((take, features, residues), lambda s: (s, 0, 0)),
            pl.BlockSpec((take, residues, features), lambda s: (s, 0, 0)),
            pl.BlockSpec((take, 1, residues), lambda s: (s, 0, 0)),
            whole(w_out.shape),
            whole((features, 128)),
            whole((side, features)),
        ],
        out_specs=[
            pl.BlockSpec((take, residues, features), lambda s: (s, 0, 0)),
            pl.BlockSpec((take, rows, 128), lambda s: (s, 0, 0)),
            whole(((side + 1) * 8, residues)),
        ],
        out_shape=[
            jax.ShapeDtypeStruct(stack.shape, BF16),
            jax.ShapeDtypeStruct((entries, rows, 128), BF16),
            jax.ShapeDtypeStruct(((side + 1) * 8, residues), BF16),
        ],
        scratch_shapes=[pltpu.VMEM(((side + 1) * 8, residues), F32)],
        compiler_params=params(16),
        name="sides",
    )(
        attended,
        gate,
        stack,
        mask[:, None, :].astype(F32),
        w_out,
        jnp.tile(w_sides[:, :side], (1, group)),
        w_sides[:, side:].T,
    )


OUTER_CHUNKS = 2


def outer_kernel(
    side, at_ref, left_ref, mine_ref, other_ref, couple_ref, live_ref, we_ref, wt_ref,
    mid_ref, pair_ref, right_ref, rmask_ref, rows_ref, x_ref, update_ref, count_ref,
):
    step = pl.program_id(0)
    rows, lanes = couple_ref.shape[0], couple_ref.shape[1]
    channels = couple_ref.shape[2]
    pair_rows = live_ref.shape[0]
    entries = rmask_ref.shape[0]

    @pl.when(step == 0)
    def _():
        length, branches = mine_ref.shape[0], mine_ref.shape[1]

        @pl.loop(0, branches * length)
        def _(plane):
            place = ring_place((plane + branches * length - at_ref[2]) % length, length)
            which = jnp.bitwise_xor(plane // length, at_ref[1])
            at = pl.ds(pl.multiple_of(plane * 16, 16), 16)
            for d in range(side + 1):
                pair = [ref[place, which, d * 8 : (d + 1) * 8] for ref in (mine_ref, other_ref)]
                pair = jnp.concatenate(pair, axis=0)
                if d < side:
                    right_ref[d // 2, at, d % 2 * lanes : (d % 2 + 1) * lanes] = pair
                else:
                    rmask_ref[at, :] = pair

        columns, tiles, members, _ = left_ref.shape
        given = lax.broadcasted_iota(jnp.int32, (entries, entries), 0)
        wanted = lax.broadcasted_iota(jnp.int32, (entries, entries), 1)
        member = jnp.bitwise_xor(given % members, at_ref[0])
        order = jnp.where(member * columns + given // members == wanted, 1.0, 0.0).astype(BF16)
        for t in range(tiles):
            rows_in = jnp.concatenate([left_ref[c, t] for c in range(columns)], axis=0)
            turned = dot(rows_in, order, (0, 0)).astype(BF16)
            if t < tiles - 1:
                rows_ref[t * 128 : (t + 1) * 128] = turned
            else:
                count_ref[...] = 1.0 / (dot(turned, rmask_ref[...], (1, 0)) + 1.0)

    @pl.when(step < OUTER_CHUNKS)
    def _():
        part = side // OUTER_CHUNKS
        for k in range(0, part, 2):
            sums = dot(rows_ref[...], right_ref[step * (part // 2) + k // 2], (1, 0)).astype(BF16)
            for i in range(pair_rows):
                for e in range(2):
                    x_ref[(k + e) * side : (k + e + 1) * side, i * lanes : (i + 1) * lanes] = sums[
                        i * side : (i + 1) * side, e * lanes : (e + 1) * lanes
                    ]
        added = dot(we_ref[step], x_ref[...], (1, 0))

        @pl.when(step == 0)
        def _():
            update_ref[...] = added

        @pl.when(step > 0)
        def _():
            update_ref[...] += added

    @pl.when(step >= OUTER_CHUNKS)
    def _():
        first = (step - OUTER_CHUNKS) * rows
        normed = []
        for i in range(rows):
            over = count_ref[pl.ds(at_ref[3] * pair_rows + first + i, 1), :]
            update = update_ref[:, pl.ds(pl.multiple_of((first + i) * lanes, lanes), lanes)]
            mid = couple_ref[i].astype(F32).T + update * over
            mid_ref[i] = mid
            normed.append(standardize(mid, 0).astype(BF16))
        normed = jnp.concatenate(normed, axis=1)
        for part in (0, 2):
            gate = dot(wt_ref[part * channels : (part + 1) * channels], normed, (1, 0))
            value = dot(wt_ref[(part + 1) * channels : (part + 2) * channels], normed, (1, 0))
            both = sigmoid(gate) * value
            for i in range(rows):
                live = live_ref[pl.ds(first + i, 1), :]
                pair_ref[i, part // 2] = (both[:, i * lanes : (i + 1) * lanes] * live).astype(BF16)


def outer(at, left, mine, other, couple, live, w_exit, w_tri):
    entries = left.shape[0] * left.shape[2]
    pair_rows, lanes, channels = couple.shape
    rows = 8
    side = mine.shape[2] // 8 - 1
    move = lambda t, at: (jnp.maximum(t - OUTER_CHUNKS, 0), 0, 0)
    tile = pl.BlockSpec((rows, channels, lanes), move)
    depth = side * side // OUTER_CHUNKS
    w_exit = w_exit.reshape(side, side, channels).transpose(1, 0, 2)
    w_exit = w_exit.reshape(OUTER_CHUNKS, depth, channels).transpose(0, 2, 1)
    return pl.pallas_call(
        functools.partial(outer_kernel, side),
        grid_spec=pltpu.PrefetchScalarGridSpec(
            num_scalar_prefetch=1,
            grid=(OUTER_CHUNKS + pair_rows // rows,),
            in_specs=[
                whole(left.shape),
                whole(mine.shape),
                whole(other.shape),
                pl.BlockSpec((rows, lanes, channels), move),
                whole(live.shape),
                whole(w_exit.shape),
                whole((4 * channels, channels)),
            ],
            out_specs=[
                tile,
                pl.BlockSpec((rows, 2, channels, lanes), lambda t, at: (*move(t, at), 0)),
            ],
            scratch_shapes=[
                pltpu.VMEM((side // 2, entries, 2 * lanes), BF16),
                pltpu.VMEM((entries, lanes), BF16),
                pltpu.VMEM((pair_rows * side, entries), BF16),
                pltpu.VMEM((depth, pair_rows * lanes), BF16),
                pltpu.VMEM((channels, pair_rows * lanes), F32),
                pltpu.VMEM((128, lanes), F32),
            ],
        ),
        out_shape=[
            jax.ShapeDtypeStruct((pair_rows, channels, lanes), F32),
            jax.ShapeDtypeStruct((pair_rows, 2, channels, lanes), BF16),
        ],
        compiler_params=params(60),
        name="outer",
    )(at, left, mine, other, couple, live, w_exit, w_tri.T)


def triangle_kernel(me_ref, l_ref, mine_ref, other_ref, out_ref):
    planes, columns, tile, lanes = l_ref.shape
    first = me_ref[0] == 0
    joined = lambda ref, p: jnp.concatenate([ref[p, k] for k in range(columns)], axis=1)
    rights = []
    for p in range(mine_ref.shape[0]):
        a, b = joined(mine_ref, p), joined(other_ref, p)
        rights += [jnp.where(first, a, b), jnp.where(first, b, a)]
    right = jnp.concatenate(rights, axis=0)
    per = lanes // (2 * tile)
    for p in range(0, planes, 4):
        left = jnp.concatenate([joined(l_ref, p + q) for q in range(4)], axis=0)
        product = dot(left, right, (1, 1)).astype(BF16)
        for q in range(4):
            for n in range(mine_ref.shape[0] // per):
                out_ref[p + q, n] = product[
                    q * tile : (q + 1) * tile, n * lanes : (n + 1) * lanes
                ]


def triangle(me, left, mine, other):
    planes, columns, tile, lanes = left.shape
    per = lanes // (2 * tile)
    take = 2
    spec = pl.BlockSpec((per * take, columns, tile, lanes), lambda n, me: (n, 0, 0, 0))
    return pl.pallas_call(
        triangle_kernel,
        grid_spec=pltpu.PrefetchScalarGridSpec(
            num_scalar_prefetch=1,
            grid=(columns // take,),
            in_specs=[whole(left.shape), spec, spec],
            out_specs=pl.BlockSpec((planes, take, tile, lanes), lambda n, me: (0, n, 0, 0)),
        ),
        out_shape=jax.ShapeDtypeStruct(left.shape, BF16),
        compiler_params=params(20),
        name="triangle",
    )(me, left, mine, other)


def switch_kernel(mid_ref, ws_ref, gate_ref):
    rows, _, lanes = mid_ref.shape
    normed = [standardize(mid_ref[i], 0).astype(BF16) for i in range(rows)]
    gate = sigmoid(dot(ws_ref[...], jnp.concatenate(normed, axis=1), (1, 0)))
    for i in range(rows):
        gate_ref[i] = gate[:, i * lanes : (i + 1) * lanes]


def switch(mid, w_switch):
    pair_rows, channels, lanes = mid.shape
    tile = pl.BlockSpec((2, channels, lanes), lambda t: (t, 0, 0))
    return pl.pallas_call(
        switch_kernel,
        grid=(pair_rows // 2,),
        in_specs=[tile, whole(w_switch.shape)],
        out_specs=tile,
        out_shape=jax.ShapeDtypeStruct(mid.shape, F32),
        compiler_params=params(16),
        name="switch",
    )(mid, w_switch.T)


def finish_kernel(prod_ref, mid_ref, gate_ref, wo_ref, out_ref, mixed_ref):
    step = pl.program_id(0)
    channels, pair_rows, lanes = prod_ref.shape
    rows = mid_ref.shape[0]

    @pl.when(step == 0)
    def _():
        zero = jnp.zeros((pair_rows, lanes), F32)
        take = 16

        def add(k, total):
            for c in range(take):
                total = total + prod_ref[k * take + c].astype(F32)
            return total

        mean = lax.fori_loop(0, channels // take, add, zero) / channels

        def add_square(k, total):
            for c in range(take):
                centered = prod_ref[k * take + c].astype(F32) - mean
                total = total + centered * centered
            return total

        spread = lax.fori_loop(0, channels // take, add_square, zero) / channels
        inverse = lax.rsqrt(spread + EPSILON)

        @pl.loop(0, channels // take)
        def _(k):
            for c in range(take):
                row = pl.multiple_of((k * take + c) * pair_rows, pair_rows)
                mixed_ref[pl.ds(row, pair_rows), :] = (
                    prod_ref[k * take + c].astype(F32) - mean
                ) * inverse

    mixed = [
        mixed_ref[pl.ds(step * rows + i, channels, stride=pair_rows), :].astype(BF16)
        for i in range(rows)
    ]
    update = dot(wo_ref[...], jnp.concatenate(mixed, axis=1), (1, 0))
    for i in range(rows):
        result = mid_ref[i] + update[:, i * lanes : (i + 1) * lanes] * gate_ref[i]
        out_ref[i] = result.T.astype(BF16)


def finish(product, mid, gate, w_out):
    channels, pair_rows, lanes = product.shape
    rows = 8
    tile = pl.BlockSpec((rows, channels, lanes), lambda t: (t, 0, 0))
    return pl.pallas_call(
        finish_kernel,
        grid=(pair_rows // rows,),
        in_specs=[whole(product.shape), tile, tile, whole(w_out.shape)],
        out_specs=pl.BlockSpec((rows, lanes, channels), lambda t: (t, 0, 0)),
        out_shape=jax.ShapeDtypeStruct((pair_rows, lanes, channels), BF16),
        scratch_shapes=[pltpu.VMEM((channels * pair_rows, lanes), F32)],
        compiler_params=params(24),
        name="finish",
    )(product, mid, gate, w_out.T)


def swap(x):
    return lax.ppermute(x, "row_1", SWAP)


def exchange(x, axes):
    return lax.all_to_all(x, axes, 0, 0, tiled=True)


def ring_gather(x):
    n = lax.axis_size("row_0")

    def shift(y, by):
        return lax.ppermute(y, "row_0", tuple((k, (k + by) % n) for k in range(n)))

    across = lax.ppermute(x, "branch", SWAP)
    pair = jnp.stack([x, across])
    above, below, above_2, below_2 = (shift(pair, by) for by in (1, -1, 2, -2))
    above_3, below_3 = shift(above_2, 1), shift(below_2, -1)
    last = [shift(above_2[:1], 2), shift(below_2[1:], -2)]
    return jnp.stack([pair, above, below, above_2, below_2, above_3, below_3, jnp.concatenate(last)])


def ring_place(ahead, n):
    return jnp.where(ahead <= n // 2, jnp.maximum(2 * ahead - (ahead == n // 2), 0), 2 * (n - ahead) - 1)


def repeated(x, n):
    return jnp.broadcast_to(x[None], (n, *x.shape))


def shards(
    homolog_stack,
    couple_tensor,
    amino_occupancy,
    homolog_occupancy,
    focus_entry_coefficients,
    couple_offset_coefficients,
    focus_exit_coefficients,
    tensor_entry_coefficients,
    tensor_exit_coefficients,
    trio_entry_coefficients,
    trio_exit_switch,
    trio_exit_coefficients,
):
    _, residues, features = homolog_stack.shape
    pair_rows, pair_cols, pair_width = couple_tensor.shape
    heads = couple_offset_coefficients.shape[1]
    width = features // heads
    side = tensor_entry_coefficients.shape[1] // 2
    planes = lax.axis_size("branch") * lax.axis_size("row_0")
    chan = lax.axis_size("chan")
    core = lax.axis_index("row_1").astype(jnp.int32)
    row = lax.axis_index(BRANCH_ROW).astype(jnp.int32)
    place = [core, lax.axis_index("branch"), lax.axis_index("row_0"), row % 4]
    at = jnp.stack([p.astype(jnp.int32) for p in place])
    me = core.reshape(1)
    live = amino_occupancy.astype(F32)
    live_rows = lax.dynamic_slice_in_dim(live, row * pair_rows, pair_rows)
    live_cols = lax.dynamic_slice_in_dim(live, lax.axis_index("chan") * pair_cols, pair_cols)
    penalty = ((live - 1.0) * MASKED)[None, :]

    bias = pair_bias(couple_tensor, couple_offset_coefficients)
    bias = exchange(bias, "chan")
    bias = ring_gather(bias)
    bias_other = swap(bias)

    qkv, gate = project_msa(homolog_stack, focus_entry_coefficients, heads)
    qkv = exchange(qkv, "chan")
    attended = attend(at, qkv, bias, bias_other, penalty, width)
    attended = exchange(attended, "chan")

    homolog_after_update, left, right = sides(
        attended,
        gate,
        homolog_stack,
        homolog_occupancy,
        focus_exit_coefficients,
        tensor_entry_coefficients,
    )
    right = ring_gather(right)
    right_other = swap(right)
    members = 2 * planes
    packed_rows = residues * side // 128
    steps = chan * packed_rows // members
    left = exchange(left, "chan")
    left = jnp.concatenate(
        [
            left[:, :packed_rows].reshape(members, steps, 128),
            jnp.repeat(left[:, packed_rows : packed_rows + 8], members // chan, axis=0),
        ],
        axis=1,
    )
    left = exchange(left, BRANCH_ROW)
    left = repeated(left[:, : steps + 1].transpose(1, 0, 2), chan)
    left = exchange(left, "chan")
    mid, operands = outer(
        at,
        left,
        right,
        right_other,
        couple_tensor,
        live_rows[:, None] * live_cols[None, :],
        tensor_exit_coefficients,
        trio_entry_coefficients,
    )
    operands = with_layout_constraint(operands.transpose(2, 1, 0, 3), Layout((0, 1, 2, 3)))
    operands = with_layout_constraint(exchange(operands, CHIPS), Layout((0, 1, 2, 3)))
    grid = (planes, chan, pair_rows, pair_cols)
    left_tri, right_tri = operands[:, 0].reshape(grid), operands[:, 1].reshape(grid)
    product = triangle(me, left_tri, right_tri, swap(right_tri))
    product = exchange(product.reshape(pair_width, pair_rows, pair_cols), CHIPS)
    gate = switch(mid, trio_exit_switch)
    pair_result = finish(product, mid, gate, trio_exit_coefficients)
    return (homolog_after_update, pair_result)


def solution(mesh):
    torus = Mesh(
        mesh.devices.reshape(mesh.shape["branch"], 8, 2, mesh.shape["chan"]),
        ("branch", "row_0", "row_1", "chan"),
    )

    return jax.shard_map(
        shards,
        mesh=torus,
        in_specs=(
            P(BRANCH_ROW, "chan", None),
            P(BRANCH_ROW, "chan", None),
            P(),
            P(BRANCH_ROW, "chan"),
            *(P() for _ in range(8)),
        ),
        out_specs=(P(BRANCH_ROW, "chan", None), P(BRANCH_ROW, "chan", None)),
        check_vma=False,
    )
```
